32 devices in a mesh: groups: 2 (over y), row: 8 (over z, x), col: 2 (over core).
Axes of the slice: x: 2, y: 2, z: 4, core: 2. Of those that a mesh axis runs over, the one named last changes fastest.
Arguments:
- concentration: float32 [512, 256, 256], P('groups', 'row', 'col'), parts along dimension 0, may hold values from -6 to 6
- species: int32 [2], P('groups'), parts along dimension 0, may hold values from 0 to 63
- reaction_rates: float32 [64], replicated, may hold values from 0.2 to 0.8
- levels: float32 [64], replicated, may hold values from -1 to 1
- sweep_flags: int32 [2, 3], replicated, may hold values from 0 to 1
- explicit_line: float32 [256, 256], replicated, may hold values from -0.5 to 1.2
- inverse_line: float32 [256, 256], replicated, may hold values from -0.5 to 1.2
- explicit_depth: float32 [256, 256], replicated, may hold values from -0.5 to 1.2
- inverse_depth: float32 [256, 256], replicated, may hold values from -0.5 to 1.2
Outputs:
- advanced: float32 [512, 256, 256], P('groups', 'row', 'col'), parts along dimension 0
The draws below stay inside these ranges and needn't reach their ends.
There are 2 independent parts, one for each index of `groups`. The reference program is written for one: setup_inputs(seed, part) draws one part's arguments, and reference() takes and returns one part's arrays. A program takes and returns all parts, laid end to end along the dimension named above; an argument that names none is the same for every part. Nothing has to cross between parts.
All inputs are finite; a program needn't handle non-finite values.
Results may differ from the reference program's by a relative error of at most 0.00011.
Values sent between devices are 32-bit elements; how exact they have to be, the bound alone decides.
A program may use at most 64 MiB of HBM per device.

```python
import math
import jax
import jax.numpy as jnp
from jax import lax

NL = 256
NZ = 256
STEPS = 2
SPECIES = 64


def build_operator(key, order_size, lowest, highest):
    key_diagonal, key_spread = jax.random.split(key)
    diagonal_part = jax.random.uniform(key_diagonal, (order_size,), jnp.float32, lowest, highest)
    spread_part = jnp.clip(jax.random.normal(key_spread, (order_size, order_size), jnp.float32), -3.0, 3.0)
    spread_part = spread_part * (0.3 / math.sqrt(order_size))
    return spread_part + jnp.diag(diagonal_part)


def draw_explicit_line(key, part):
    return build_operator(jax.random.fold_in(key, 11), NL, 0.9, 1.1)


def draw_inverse_line(key, part):
    return build_operator(jax.random.fold_in(key, 23), NL, 0.8, 1.0)


def draw_explicit_depth(key, part):
    return build_operator(jax.random.fold_in(key, 37), NZ, 0.9, 1.1)


def draw_inverse_depth(key, part):
    return build_operator(jax.random.fold_in(key, 41), NZ, 0.8, 1.0)


def touch_ends(result, stream_key, low, high):
    longest = result.shape.index(max(result.shape))
    spots = []
    for shift in (0, 1):
        where = [jax.random.randint(jax.random.fold_in(stream_key, axis), (), 0, length) for axis, length in enumerate(result.shape)]
        where[longest] = (where[longest] + shift) % result.shape[longest]
        spots.append(tuple(where))
    return result.at[spots[0]].set(low).at[spots[1]].set(high)


def block_scale(rng, dims, shards, least, high):
    def one(dim, parts):
        heights = jax.random.uniform(jax.random.fold_in(jax.random.fold_in(rng, 6), dim), (parts,), jnp.float32, least / len(shards), high / len(shards))
        return jnp.repeat(jnp.exp(heights), dims[dim] // parts).reshape((-1,) + (1,) * (len(dims) - dim - 1))

    factor_of = one(*shards[0])
    for cut in shards[1:]:
        factor_of = factor_of * one(*cut)
    return factor_of


def noise(key, dims, width, bound, shards=(), held_as=jnp.bfloat16):
    values = jax.random.normal(key, dims, jnp.float32) * width
    if len(shards) > 0:
        values = block_scale(key, dims, shards, -0.22, 0.18) * values
    return jnp.clip(values, min=-bound, max=bound).astype(held_as)


def setup_inputs(seed: int = 0, part: int = 0) -> dict:
    key_list = jax.random.split(jax.random.key(seed), 10)
    own_keys = jax.random.split(jax.random.fold_in(key_list[9], part), 10)
    return {
        "concentration": noise(own_keys[0], (NL, NL, NZ), 1.0, 6.0, ((1, 8), (2, 2)), jnp.float32),
        "species": jax.random.randint(own_keys[1], (1,), 0, SPECIES).astype(jnp.int32),
        "reaction_rates": jnp.clip(jnp.exp(jax.random.uniform(key_list[2], (SPECIES,), jnp.float32, math.log(0.2), math.log(0.8))), 0.2, 0.8),
        "levels": jnp.clip(jax.random.uniform(key_list[3], (SPECIES,), jnp.float32, -1.0, 1.0), -1.0, 1.0),
        "sweep_flags": touch_ends(jax.random.randint(key_list[4], (STEPS, 3), 0, 2), jax.random.fold_in(key_list[4], 1), 0, 1).astype(jnp.int32),
        "explicit_line": draw_explicit_line(jax.random.fold_in(key_list[9], 71), part),
        "inverse_line": draw_inverse_line(jax.random.fold_in(key_list[9], 71), part),
        "explicit_depth": draw_explicit_depth(jax.random.fold_in(key_list[9], 71), part),
        "inverse_depth": draw_inverse_depth(jax.random.fold_in(key_list[9], 71), part),
    }


def apply_line(matrix, field_now, axis_dim):
    if axis_dim == 0:
        return jnp.einsum("ij,jbc->ibc", matrix, field_now, precision=lax.Precision.HIGHEST)
    if axis_dim == 1:
        return jnp.einsum("ij,ajc->aic", matrix, field_now, precision=lax.Precision.HIGHEST)
    return jnp.einsum("ij,abj->abi", matrix, field_now, precision=lax.Precision.HIGHEST)


def oriented(matrix, reflect):
    return jnp.where(reflect == 1, matrix[::-1, ::-1], matrix)


def reference(concentration, species, reaction_rates, levels, sweep_flags, explicit_line, inverse_line, explicit_depth, inverse_depth):
    picker = (jnp.arange(reaction_rates.shape[0], dtype=jnp.int32) == species[0]).astype(jnp.float32)
    kinetic_rate = jnp.sum(reaction_rates * picker)
    equilibrium = jnp.sum(levels * picker)
    field_now = concentration
    for step_index in range(STEPS):
        order = [0, 1, 2] if step_index % 2 == 0 else [2, 1, 0]
        for axis_dim in order:
            if axis_dim < 2:
                explicit_now, inverse_now = explicit_line, inverse_line
            else:
                explicit_now, inverse_now = explicit_depth, inverse_depth
            reflect = sweep_flags[step_index, axis_dim]
            field_now = field_now - kinetic_rate * jnp.tanh(field_now - equilibrium)
            field_now = apply_line(oriented(explicit_now, reflect), field_now, axis_dim)
            field_now = apply_line(oriented(inverse_now, reflect), field_now, axis_dim)
    return field_now
```

```python
import functools

import jax
import jax.numpy as jnp
import numpy as np
from jax import lax
from jax.experimental import pallas as pl
from jax.experimental.pallas import tpu as pltpu
from jax.sharding import PartitionSpec as P

MESH = pl.DeviceIdType.MESH
LANES = 128


def react(v, rate, level):
    return v - rate * jnp.tanh(v - level)


def split(v):
    hi = v.astype(jnp.bfloat16)
    lo = (v - hi.astype(jnp.float32)).astype(jnp.bfloat16)
    return hi, lo


def dot3(a, b):
    (ah, al), (bh, bl) = a, b
    dot = functools.partial(jnp.dot, preferred_element_type=jnp.float32)
    return dot(ah, bh) + (dot(ah, bl) + dot(al, bh))


def load_columns(ref, r, width, start, lines):
    rows, lanes = ref.shape[1:]
    if rows % 8 == 0:
        flat = ref.reshape(ref.shape[0] * rows, lanes)
        parts = [flat[pl.ds(start * rows + r + i, lines, stride=rows), :] for i in range(width)]
    else:
        parts = [ref[start : start + lines, r + i, :] for i in range(width)]
    return jnp.concatenate(parts, axis=1)


def store_columns(ref, r, width, value):
    lines, rows, lanes = ref.shape
    for i in range(width):
        part = value[:, i * lanes : (i + 1) * lanes]
        if rows % 8 == 0:
            flat = ref.reshape(lines * rows, lanes)
            flat[pl.ds(r + i, lines, stride=rows), :] = part
        else:
            ref[:, r + i, :] = part


def move(source, target):
    return jnp.dot(source, target, preferred_element_type=jnp.float32).astype(jnp.bfloat16)


def orientations(matrix):
    size = matrix.shape[0]
    i = lax.broadcasted_iota(jnp.int32, (size, size), 0)
    j = lax.broadcasted_iota(jnp.int32, (size, size), 1)
    exchange = jnp.where(i + j == size - 1, 1.0, 0.0).astype(jnp.bfloat16)
    halves = split(matrix)
    return halves, tuple(move(move(exchange, m), exchange) for m in halves)


def choose(flag, plain, turned):
    where = jnp.full(plain[0].shape, flag, jnp.int32) == 1
    return tuple(
        jnp.where(where, b.astype(jnp.float32), a.astype(jnp.float32)).astype(jnp.bfloat16)
        for a, b in zip(plain, turned)
    )


def fold(inverse, explicit, transposed):
    if transposed:
        inverse, explicit = explicit.T, inverse.T
    return dot3(split(inverse), split(explicit))


def sweep_columns(matrix, source, target, rate, level):
    lines, rows, _ = source.shape
    cols = 2 if rows % 2 == 0 else 1
    for r in range(0, rows, cols):
        k = split(react(load_columns(source, r, cols, 0, lines), rate, level))
        store_columns(target, r, cols, dot3(matrix, k))


def kernel(
    n, L, R, C, G,
    species, rates_hbm, levels_hbm, flags_hbm, e_line_hbm, p_line_hbm, e_depth_hbm, p_depth_hbm, x_hbm,
    *refs,
):
    done, refs = (refs[0], refs[1:]) if G > 1 else (None, refs)
    (
        raw, lead, pair_out,
        rates, levels, flags, e_line, p_line, e_depth, p_depth,
        x, y, z, w, v, h, t, u, f, mh, ml,
        x_sem, in_sem, own1, own2, send1, recv1, send2, recv2, recv3, a_send, a_recv, b_send, b_recv, o_sem,
    ) = refs
    me = lax.axis_index("row")
    q = lax.axis_index("col")
    per = L // C
    pair = 2 if per % 2 == 0 else 1
    group = R // G

    inputs = [
        pltpu.make_async_copy(source, target, in_sem.at[i])
        for i, (source, target) in enumerate(
            (
                (p_line_hbm, p_line), (e_line_hbm, e_line), (rates_hbm, rates),
                (levels_hbm, levels), (flags_hbm, flags), (p_depth_hbm, p_depth), (e_depth_hbm, e_depth),
            )
        )
    ]

    def x_copy(g):
        return pltpu.make_async_copy(x_hbm.at[:, pl.ds(g * group, group)], x.at[g], x_sem.at[g])

    for copy in inputs[:5]:
        copy.start()
    for g in range(G):
        x_copy(g).start()
    for copy in inputs[5:]:
        copy.start()

    barrier = pltpu.get_barrier_semaphore()

    def greet(j, carry):
        pl.semaphore_signal(
            barrier, inc=1, device_id={"row": lax.rem(me + j, n)}, device_id_type=MESH
        )
        return carry

    lax.fori_loop(1, n, greet, 0, unroll=n <= 8)
    pl.semaphore_signal(barrier, inc=1, device_id={"col": 1 - q}, device_id_type=MESH)

    for copy in inputs[:5]:
        copy.wait()
    kind = species[0]
    rate, level = rates[kind], levels[kind]

    def keep(slot, flag, plain, turned):
        mh[slot], ml[slot] = choose(flag, plain, turned)

    def around(body):
        def turn(j, carry):
            body(lax.rem(me + j, n))
            return carry

        lax.fori_loop(1, n, turn, 0, unroll=n <= 8)

    def send_rows(c, groups):
        def send_to(d):
            for g in groups:
                pltpu.make_async_remote_copy(
                    src_ref=y.at[g, pl.ds(d * L + c * per, per)],
                    dst_ref=z.at[pl.ds(c * per, per), me, pl.ds(g * group, group)],
                    send_sem=send1,
                    recv_sem=recv1.at[c],
                    device_id={"row": d},
                    device_id_type=MESH,
                ).start()

        around(send_to)

    lines = orientations(fold(p_line[...], e_line[...], False))
    first = choose(flags[0, 0], *lines)
    x_copy(0).wait()
    sweep_columns(first, x.at[0], y.at[0], rate, level)
    pl.semaphore_wait(barrier, n)
    send_rows(0, (0,))
    mh[0], ml[0] = first
    for g in range(1, G):
        x_copy(g).wait()
        sweep_columns((mh[0], ml[0]), x.at[g], y.at[g], rate, level)
    if G > 1:
        send_rows(0, range(1, G))

    def own_copy(c, g):
        return pltpu.make_async_copy(
            y.at[g, pl.ds(me * L + c * per, per)],
            z.at[pl.ds(c * per, per), me, pl.ds(g * group, group)],
            own1.at[c, g],
        )

    def send_chunk(c, carry):
        send_rows(c, range(G))
        for g in range(G):
            own_copy(c, g).start()
        return carry

    for g in range(G):
        own_copy(0, g).start()
    lax.fori_loop(1, C, send_chunk, 0)

    for copy in inputs[5:]:
        copy.wait()
    keep(1, flags[0, 1], *lines)
    keep(4, flags[1, 1], *lines)
    lead[0], lead[1] = choose(flags[1, 0], *lines)
    pair_out[0] = jnp.full(pair_out.shape[1:], rate, jnp.float32)
    pair_out[1] = jnp.full(pair_out.shape[1:], level, jnp.float32)
    depths = orientations(fold(p_depth[...], e_depth[...], True))
    keep(2, flags[0, 2], *depths)
    keep(3, flags[1, 2], *depths)

    half = n * R // 2
    mine = pl.ds(pl.multiple_of(q * half, half), half)
    theirs = pl.ds(pl.multiple_of((1 - q) * half, half), half)
    lanes_mine = pl.ds(pl.multiple_of(q * LANES, LANES), LANES)
    lanes_theirs = pl.ds(pl.multiple_of((1 - q) * LANES, LANES), LANES)
    peer = {"col": 1 - q}

    def lines_at(c):
        return pl.ds(me * L + c * per, per)

    def own_back(c, g):
        target = f.at[g] if g < G - 1 else raw
        source = u.at[pl.ds(c * per, per), me, pl.ds(g * group, group)]
        return pltpu.make_async_copy(source, target.at[lines_at(c)], own2.at[c, g])

    def chunk(c, carry):
        at = pl.ds(c * per, per)
        arrived = z.at[at, pl.ds(0, n - 1)]
        pltpu.make_async_copy(arrived, arrived, recv1.at[c]).wait()
        for g in range(G):
            own_copy(c, g).wait()

        line = tuple(jnp.concatenate([m[1, mine, :], m[1, theirs, :]], axis=0) for m in (mh, ml))
        for s in range(0, per, pair):
            i = c * per + s
            k = jnp.concatenate([z[i + e].reshape(n * R, LANES) for e in range(pair)], axis=1)
            out = dot3(line, split(react(k, rate, level)))
            for e in range(pair):
                part = out[:, e * LANES : (e + 1) * LANES]
                v[i + e, :, lanes_mine] = part[:half]
                w[i + e] = part[half:]
        to_peer = pltpu.make_async_remote_copy(
            src_ref=w.at[at],
            dst_ref=v.at[at, :, lanes_mine],
            send_sem=a_send.at[c],
            recv_sem=a_recv.at[c],
            device_id=peer,
            device_id_type=MESH,
        )
        to_peer.start()
        to_peer.wait()

        k = v[at].reshape(per * half, 2 * LANES)
        k = dot3(split(react(k, rate, level)), (mh[2], ml[2]))
        depth = tuple(
            jnp.concatenate([m[3, :, lanes_mine], m[3, :, lanes_theirs]], axis=1) for m in (mh, ml)
        )
        k = dot3(split(react(k, rate, level)), depth)
        t[at, mine, :] = k[:, :LANES].reshape(per, half, LANES)
        h[at] = k[:, LANES:].reshape(per, half, LANES)
        to_peer = pltpu.make_async_remote_copy(
            src_ref=h.at[at],
            dst_ref=t.at[at, mine, :],
            send_sem=b_send.at[c],
            recv_sem=b_recv.at[c],
            device_id=peer,
            device_id_type=MESH,
        )
        to_peer.start()
        to_peer.wait()

        line = (mh[4], ml[4])
        for s in range(0, per, pair):
            i = c * per + s
            k = jnp.concatenate([t[i + e] for e in range(pair)], axis=1)
            out = dot3(line, split(react(k, rate, level)))
            for e in range(pair):
                u[i + e] = out[:, e * LANES : (e + 1) * LANES].reshape(n, R, LANES)

        def send_back(g, recv, d):
            target = f.at[g] if g < G - 1 else raw
            pltpu.make_async_remote_copy(
                src_ref=u.at[at, d, pl.ds(g * group, group)],
                dst_ref=target.at[lines_at(c)],
                send_sem=send2,
                recv_sem=recv,
                device_id={"row": d},
                device_id_type=MESH,
            ).start()

        @pl.when(c < C - 1)
        def _():
            def send_to(d):
                for g in range(G):
                    send_back(g, recv2.at[c], d)

            around(send_to)

        @pl.when(c == C - 1)
        def _():
            for g in range(G):
                around(functools.partial(send_back, g, recv3.at[g]))

        for g in range(G):
            own_back(c, g).start()
        return carry

    lax.fori_loop(0, C, chunk, 0)

    def own_wait(c, carry):
        for g in range(G):
            own_back(c, g).wait()
        return carry

    lax.fori_loop(0, C, own_wait, 0)

    def wait_back(c, carry):
        arrived = z.at[pl.ds(0, per), pl.ds(0, n - 1)]
        pltpu.make_async_copy(arrived, arrived, recv2.at[c]).wait()
        return carry

    lax.fori_loop(0, C - 1, wait_back, 0)

    def done_copy(g):
        return pltpu.make_async_copy(x.at[g], done.at[g], o_sem.at[g])

    for g in range(G - 1):
        arrived = raw.at[pl.ds(0, (n - 1) * per)]
        pltpu.make_async_copy(arrived, arrived, recv3.at[g]).wait()
        sweep_columns((lead[0], lead[1]), f.at[g], x.at[g], rate, level)
        done_copy(g).start()
    for g in range(G - 1):
        done_copy(g).wait()
    away = z.at[:, pl.ds(0, n - 1)]
    pltpu.make_async_copy(away, away, send1).wait()
    pltpu.make_async_copy(away, away, send2).wait()
    arrived = raw.at[pl.ds(0, (n - 1) * per)]
    pltpu.make_async_copy(arrived, arrived, recv3.at[G - 1]).wait()


def last_kernel(lead, pair_in, raw, *refs):
    *done, o, out, sem = refs
    lines, group, lanes = raw.shape
    G = o.shape[1] // group

    def o_copy(g):
        source = done[0].at[g] if g < G - 1 else out
        return pltpu.make_async_copy(source, o.at[:, pl.ds(g * group, group)], sem.at[g])

    for g in range(G - 1):
        o_copy(g).start()
    cols = 2 if group % 2 == 0 else 1
    rate, level = (jnp.concatenate([pair_in[i, 0:1, :]] * cols, axis=1) for i in range(2))
    sweep_columns((lead[0], lead[1]), raw, out, rate, level)
    o_copy(G - 1).start()
    for g in range(G):
        o_copy(g).wait()


def on_device(
    n,
    concentration,
    species,
    reaction_rates,
    levels,
    sweep_flags,
    explicit_line,
    inverse_line,
    explicit_depth,
    inverse_depth,
):
    lines, R, lanes = concentration.shape
    L = lines // n
    C = max(2, L // 16)
    G = max(1, R // 8)
    per = L // C
    half = n * R // 2
    group = R // G
    f32, bf16 = jnp.float32, jnp.bfloat16

    any_spec = pl.BlockSpec(memory_space=pl.ANY)
    hbm = pl.BlockSpec(memory_space=pltpu.HBM)
    vmem = pl.BlockSpec(memory_space=pltpu.VMEM)
    dma = pltpu.SemaphoreType.DMA
    whole = jax.ShapeDtypeStruct(concentration.shape, f32)
    args = (
        reaction_rates, levels, sweep_flags,
        explicit_line, inverse_line, explicit_depth, inverse_depth,
    )
    out_shape = [
        jax.ShapeDtypeStruct((lines, group, lanes), f32),
        jax.ShapeDtypeStruct((2, lines, lines), bf16),
        jax.ShapeDtypeStruct((2, 8, lanes), f32),
    ]
    out_specs = [any_spec, vmem, vmem]
    if G > 1:
        out_shape.insert(0, jax.ShapeDtypeStruct((G - 1, lines, group, lanes), f32))
        out_specs.insert(0, any_spec)
    *done, raw, lead, pair_out = pl.pallas_call(
        functools.partial(kernel, n, L, R, C, G),
        out_shape=out_shape,
        in_specs=[pl.BlockSpec(memory_space=pltpu.SMEM)] + [hbm] * 8,
        out_specs=out_specs,
        scratch_shapes=[
            *(pltpu.SMEM(a.shape, a.dtype) for a in args[:3]),
            *(pltpu.VMEM(a.shape, a.dtype) for a in args[3:]),
            pltpu.VMEM((G, lines, group, lanes), f32),
            pltpu.VMEM((G, lines, group, lanes), f32),
            pltpu.VMEM((L, n, R, lanes), f32),
            pltpu.VMEM((L, half, lanes), f32),
            pltpu.VMEM((L, half, 2 * lanes), f32),
            pltpu.VMEM((L, half, lanes), f32),
            pltpu.VMEM((L, 2 * half, lanes), f32),
            pltpu.VMEM((L, n, R, lanes), f32),
            pltpu.VMEM((max(1, G - 1), lines, group, lanes), f32),
            pltpu.VMEM((5, lines, lines), bf16),
            pltpu.VMEM((5, lines, lines), bf16),
            dma((G,)),
            dma((7,)),
            dma((C, G)),
            dma((C, G)),
            dma,
            dma((C,)),
            dma,
            dma((C,)),
            dma((G,)),
            dma((C,)),
            dma((C,)),
            dma((C,)),
            dma((C,)),
            dma((G,)),
        ],
        compiler_params=pltpu.CompilerParams(
            collective_id=0, has_side_effects=True, vmem_limit_bytes=42 << 20
        ),
    )(species, *(pltpu.with_memory_space_constraint(a, pltpu.HBM) for a in (*args, concentration)))

    return pl.pallas_call(
        last_kernel,
        out_shape=whole,
        in_specs=[vmem] * 3 + [any_spec] * len(done),
        out_specs=hbm,
        scratch_shapes=[pltpu.VMEM((lines, group, lanes), f32), dma((G,))],
        compiler_params=pltpu.CompilerParams(vmem_limit_bytes=8 << 20),
    )(lead, pair_out, raw, *done)


def solution(mesh):
    in_specs = (P("groups", "row", "col"), P("groups"), P(), P(), P(), P(), P(), P(), P())
    out_specs = P("groups", "row", "col")
    return jax.shard_map(
        functools.partial(on_device, mesh.shape["row"]),
        mesh=mesh, in_specs=in_specs, out_specs=out_specs, check_vma=False,
    )
```

```python
import functools

import jax
import jax.numpy as jnp
import numpy as np
from jax import lax
from jax.experimental import pallas as pl
from jax.experimental.pallas import tpu as pltpu
from jax.sharding import PartitionSpec as P

MESH = pl.DeviceIdType.MESH
LANES = 128


def react(v, rate, level):
    return v - rate * jnp.tanh(v - level)


def split(v):
    hi = v.astype(jnp.bfloat16)
    lo = (v - hi.astype(jnp.float32)).astype(jnp.bfloat16)
    return hi, lo


def dot3(a, b):
    (ah, al), (bh, bl) = a, b
    dot = functools.partial(jnp.dot, preferred_element_type=jnp.float32)
    return dot(ah, bh) + (dot(ah, bl) + dot(al, bh))


def load_columns(ref, r, width, start, lines):
    rows, lanes = ref.shape[1:]
    if rows % 8 == 0:
        flat = ref.reshape(ref.shape[0] * rows, lanes)
        parts = [flat[pl.ds(start * rows + r + i, lines, stride=rows), :] for i in range(width)]
    else:
        parts = [ref[start : start + lines, r + i, :] for i in range(width)]
    return jnp.concatenate(parts, axis=1)


def store_columns(ref, r, width, value):
    lines, rows, lanes = ref.shape
    for i in range(width):
        part = value[:, i * lanes : (i + 1) * lanes]
        if rows % 8 == 0:
            flat = ref.reshape(lines * rows, lanes)
            flat[pl.ds(r + i, lines, stride=rows), :] = part
        else:
            ref[:, r + i, :] = part


def move(source, target):
    return jnp.dot(source, target, preferred_element_type=jnp.float32).astype(jnp.bfloat16)


def exchange_matrix(size):
    i = lax.broadcasted_iota(jnp.int32, (size, size), 0)
    j = lax.broadcasted_iota(jnp.int32, (size, size), 1)
    return jnp.where(i + j == size - 1, 1.0, 0.0).astype(jnp.bfloat16)


def orientations(matrix, exchange):
    halves = split(matrix)
    return halves, tuple(move(move(exchange, m), exchange) for m in halves)


def choose(flag, plain, turned):
    where = jnp.full(plain[0].shape, flag, jnp.int32) == 1
    return tuple(
        jnp.where(where, b.astype(jnp.float32), a.astype(jnp.float32)).astype(jnp.bfloat16)
        for a, b in zip(plain, turned)
    )


def fold(inverse, explicit, transposed):
    if transposed:
        inverse, explicit = explicit.T, inverse.T
    return dot3(split(inverse), split(explicit))


def sweep_columns(matrix, source, target, rate, level, blocks=None):
    lines, rows, _ = source.shape
    cols = 2 if rows % 2 == 0 else 1
    for r in range(0, rows, cols):
        k = split(react(load_columns(source, r, cols, 0, lines), rate, level))
        out, at = dot3(matrix, k), 0
        for start, count in blocks or [(0, lines)]:
            store_columns(target.at[pl.ds(start, count)], r, cols, out[at : at + count])
            at += count


def kernel(
    n, L, R, C, G,
    species, rates_hbm, levels_hbm, flags_hbm, e_line_hbm, p_line_hbm, e_depth_hbm, p_depth_hbm, x_hbm,
    *refs,
):
    done, refs = (refs[0], refs[1:]) if G > 1 else (None, refs)
    (
        raw, lead_out, pair_out,
        rates, levels, flags, mats, flip,
        x, y, z, w, v, h, t, u, f, mh, ml, lead, scalars,
        x_sem, in_sem, mat_sem, own1, own2, send1, recv1, send2, recv2, recv3, a_send, a_recv, b_send, b_recv, o_sem, pass_sem,
    ) = refs
    me = lax.axis_index("row")
    q = lax.axis_index("col")
    per = L // C
    pair = 2 if per % 2 == 0 else 1
    group = R // G

    barrier = pltpu.get_barrier_semaphore()

    def mat_copies(pair):
        sources = ((p_line_hbm, e_line_hbm), (p_depth_hbm, e_depth_hbm))[pair]
        return [
            pltpu.make_async_copy(source, mats.at[2 * pair + i], mat_sem.at[pair])
            for i, source in enumerate(sources)
        ]

    def mat_wait(pair):
        both = mats.at[pl.ds(2 * pair, 2)]
        pltpu.make_async_copy(both, both, mat_sem.at[pair]).wait()

    def x_copy(g):
        return pltpu.make_async_copy(
            x_hbm.at[:, pl.ds(g * group, group)], x.at[g], x_sem.at[min(g, 1)]
        )

    small = [
        pltpu.make_async_copy(source, target, in_sem.at[i])
        for i, (source, target) in enumerate(
            ((flags_hbm, flags), (rates_hbm, rates), (levels_hbm, levels))
        )
    ]
    for copy in [*mat_copies(0), *small, x_copy(0)]:
        copy.start()

    def greet(j, carry):
        pl.semaphore_signal(
            barrier, inc=1, device_id={"row": lax.rem(me + j, n)}, device_id_type=MESH
        )
        return carry

    lax.fori_loop(n // 2, n, greet, 0, unroll=n <= 8)
    lax.fori_loop(1, n // 2, greet, 0, unroll=n <= 8)
    pl.semaphore_signal(barrier, inc=1, device_id={"col": 1 - q}, device_id_type=MESH)

    flip[...] = exchange_matrix(n * L)

    def keep(slot, flag, plain, turned):
        mh[slot], ml[slot] = choose(flag, plain, turned)

    def around(body):
        def turn(j, carry):
            body(lax.rem(me + j, n))
            return carry

        lax.fori_loop(1, n, turn, 0, unroll=n <= 8)

    def send_rows(c, groups):
        def send_to(d):
            for g in groups:
                pltpu.make_async_remote_copy(
                    src_ref=y.at[g, pl.ds(d * L + c * per, per)],
                    dst_ref=z.at[pl.ds(c * per, per), me, pl.ds(g * group, group)],
                    send_sem=send1,
                    recv_sem=recv1.at[c],
                    device_id={"row": d},
                    device_id_type=MESH,
                ).start()

        around(send_to)

    def rows_of(matrix, blocks):
        if len(blocks) == 1:
            return matrix
        return jnp.concatenate([matrix[start : start + count] for start, count in blocks], axis=0)

    if per % 16 == 0:
        ahead = [(d * L, per) for d in range(n)]
        behind = [(d * L + per, L - per) for d in range(n)]
    else:
        ahead, behind = [(0, n * L)], []

    mat_wait(0)
    for copy in [*(x_copy(g) for g in range(1, G)), *mat_copies(1)]:
        copy.start()
    p, e = split(mats[0]), split(mats[1])
    turned_p = tuple(move(rows_of(flip[...], ahead), m) for m in p)
    turned_e = tuple(move(m, flip[...]) for m in e)
    for copy in small:
        copy.wait()
    kind = species[0]
    rate, level = rates[kind], levels[kind]
    p = choose(flags[0, 0], tuple(rows_of(m, ahead) for m in p), turned_p)
    e = choose(flags[0, 0], e, turned_e)
    first = split(dot3(p, e))
    pltpu.make_async_copy(x.at[0], x.at[0], x_sem.at[0]).wait()
    sweep_columns(first, x.at[0], y.at[0], rate, level, ahead)
    pl.semaphore_wait(barrier, n)
    send_rows(0, (0,))
    lines = orientations(fold(mats[0], mats[1], False), flip[...])
    keep(0, flags[0, 0], *lines)
    if behind:
        first = tuple(rows_of(m[0], behind) for m in (mh, ml))
        sweep_columns(first, x.at[0], y.at[0], rate, level, behind)
    if G > 1:
        rest = x.at[pl.ds(1, G - 1)]
        pltpu.make_async_copy(rest, rest, x_sem.at[1]).wait()
    for g in range(1, G):
        sweep_columns((mh[0], ml[0]), x.at[g], y.at[g], rate, level)
    if G > 1:
        send_rows(0, range(1, G))

    def own_copy(c, g):
        return pltpu.make_async_copy(
            y.at[g, pl.ds(me * L + c * per, per)],
            z.at[pl.ds(c * per, per), me, pl.ds(g * group, group)],
            own1.at[c],
        )

    def send_chunk(c, carry):
        send_rows(c, range(G))
        for g in range(G):
            own_copy(c, g).start()
        return carry

    for g in range(G):
        own_copy(0, g).start()
    lax.fori_loop(1, C, send_chunk, 0)

    mat_wait(1)
    keep(1, flags[0, 1], *lines)
    keep(4, flags[1, 1], *lines)
    lead[0], lead[1] = choose(flags[1, 0], *lines)
    scalars[0] = jnp.full(scalars.shape[1:], rate, jnp.float32)
    scalars[1] = jnp.full(scalars.shape[1:], level, jnp.float32)
    passed = [
        pltpu.make_async_copy(source, target, pass_sem.at[i])
        for i, (source, target) in enumerate(((lead, lead_out), (scalars, pair_out)))
    ]
    for copy in passed:
        copy.start()
    depths = orientations(fold(mats[2], mats[3], True), flip[...])
    keep(2, flags[0, 2], *depths)
    keep(3, flags[1, 2], *depths)

    half = n * R // 2
    mine = pl.ds(pl.multiple_of(q * half, half), half)
    theirs = pl.ds(pl.multiple_of((1 - q) * half, half), half)
    lanes_mine = pl.ds(pl.multiple_of(q * LANES, LANES), LANES)
    lanes_theirs = pl.ds(pl.multiple_of((1 - q) * LANES, LANES), LANES)
    peer = {"col": 1 - q}

    def lines_at(c):
        return pl.ds(me * L + c * per, per)

    def own_back(c, g):
        target = f.at[g] if g < G - 1 else raw
        source = u.at[pl.ds(c * per, per), me, pl.ds(g * group, group)]
        return pltpu.make_async_copy(source, target.at[lines_at(c)], own2)

    def chunk(c, carry):
        at = pl.ds(c * per, per)
        arrived = z.at[at, pl.ds(0, n - 1)]
        pltpu.make_async_copy(arrived, arrived, recv1.at[c]).wait()
        own = z.at[at, me]
        pltpu.make_async_copy(own, own, own1.at[c]).wait()

        line = tuple(jnp.concatenate([m[1, mine, :], m[1, theirs, :]], axis=0) for m in (mh, ml))
        for s in range(0, per, pair):
            i = c * per + s
            k = jnp.concatenate([z[i + e].reshape(n * R, LANES) for e in range(pair)], axis=1)
            out = dot3(line, split(react(k, rate, level)))
            for e in range(pair):
                part = out[:, e * LANES : (e + 1) * LANES]
                v[i + e, :, lanes_mine] = part[:half]
                w[i + e] = part[half:]
        to_peer = pltpu.make_async_remote_copy(
            src_ref=w.at[at],
            dst_ref=v.at[at, :, lanes_mine],
            send_sem=a_send,
            recv_sem=a_recv,
            device_id=peer,
            device_id_type=MESH,
        )
        to_peer.start()
        to_peer.wait()

        k = v[at].reshape(per * half, 2 * LANES)
        k = dot3(split(react(k, rate, level)), (mh[2], ml[2]))
        depth = tuple(
            jnp.concatenate([m[3, :, lanes_mine], m[3, :, lanes_theirs]], axis=1) for m in (mh, ml)
        )
        k = dot3(split(react(k, rate, level)), depth)
        t[at, mine, :] = k[:, :LANES].reshape(per, half, LANES)
        h[at] = k[:, LANES:].reshape(per, half, LANES)
        to_peer = pltpu.make_async_remote_copy(
            src_ref=h.at[at],
            dst_ref=t.at[at, mine, :],
            send_sem=b_send,
            recv_sem=b_recv,
            device_id=peer,
            device_id_type=MESH,
        )
        to_peer.start()
        to_peer.wait()

        line = (mh[4], ml[4])
        for s in range(0, per, pair):
            i = c * per + s
            k = jnp.concatenate([t[i + e] for e in range(pair)], axis=1)
            out = dot3(line, split(react(k, rate, level)))
            for e in range(pair):
                u[i + e] = out[:, e * LANES : (e + 1) * LANES].reshape(n, R, LANES)

        def send_back(g, recv, d):
            target = f.at[g] if g < G - 1 else raw
            pltpu.make_async_remote_copy(
                src_ref=u.at[at, d, pl.ds(g * group, group)],
                dst_ref=target.at[lines_at(c)],
                send_sem=send2,
                recv_sem=recv,
                device_id={"row": d},
                device_id_type=MESH,
            ).start()

        @pl.when(c < C - 1)
        def _():
            def send_to(d):
                for g in range(G):
                    send_back(g, recv2.at[c], d)

            around(send_to)

        @pl.when(c == C - 1)
        def _():
            for g in range(G):
                around(functools.partial(send_back, g, recv3.at[g]))

        for g in range(G):
            own_back(c, g).start()
        return carry

    lax.fori_loop(0, C, chunk, 0)
    for copy in passed:
        copy.wait()

    own = z.at[:, me]
    pltpu.make_async_copy(own, own, own2).wait()

    def wait_back(c, carry):
        arrived = z.at[pl.ds(0, per), pl.ds(0, n - 1)]
        pltpu.make_async_copy(arrived, arrived, recv2.at[c]).wait()
        return carry

    lax.fori_loop(0, C - 1, wait_back, 0)

    def done_copy(g):
        return pltpu.make_async_copy(x.at[g], done.at[g], o_sem)

    for g in range(G - 1):
        arrived = raw.at[pl.ds(0, (n - 1) * per)]
        pltpu.make_async_copy(arrived, arrived, recv3.at[g]).wait()
        sweep_columns((lead[0], lead[1]), f.at[g], x.at[g], rate, level)
        done_copy(g).start()
    if G > 1:
        pltpu.make_async_copy(done, done, o_sem).wait()
    away = z.at[:, pl.ds(0, n - 1)]
    pltpu.make_async_copy(away, away, send1).wait()
    pltpu.make_async_copy(away, away, send2).wait()
    arrived = raw.at[pl.ds(0, (n - 1) * per)]
    pltpu.make_async_copy(arrived, arrived, recv3.at[G - 1]).wait()


def last_kernel(lead, pair_in, raw, *refs):
    *done, o, out, sem = refs
    lines, group, lanes = raw.shape
    G = o.shape[1] // group

    def o_copy(g):
        source = done[0].at[g] if g < G - 1 else out
        return pltpu.make_async_copy(source, o.at[:, pl.ds(g * group, group)], sem.at[g])

    for g in range(G - 1):
        o_copy(g).start()
    cols = 2 if group % 2 == 0 else 1
    rate, level = (jnp.concatenate([pair_in[i, 0:1, :]] * cols, axis=1) for i in range(2))
    sweep_columns((lead[0], lead[1]), raw, out, rate, level)
    o_copy(G - 1).start()
    for g in range(G):
        o_copy(g).wait()


def on_device(
    n,
    concentration,
    species,
    reaction_rates,
    levels,
    sweep_flags,
    explicit_line,
    inverse_line,
    explicit_depth,
    inverse_depth,
):
    lines, R, lanes = concentration.shape
    L = lines // n
    C = max(2, L // 16)
    G = max(1, R // 8)
    per = L // C
    half = n * R // 2
    group = R // G
    f32, bf16 = jnp.float32, jnp.bfloat16

    any_spec = pl.BlockSpec(memory_space=pl.ANY)
    hbm = pl.BlockSpec(memory_space=pltpu.HBM)
    vmem = pl.BlockSpec(memory_space=pltpu.VMEM)
    dma = pltpu.SemaphoreType.DMA
    whole = jax.ShapeDtypeStruct(concentration.shape, f32)
    args = (
        reaction_rates, levels, sweep_flags,
        explicit_line, inverse_line, explicit_depth, inverse_depth,
    )
    out_shape = [
        jax.ShapeDtypeStruct((lines, group, lanes), f32),
        jax.ShapeDtypeStruct((2, lines, lines), bf16),
        jax.ShapeDtypeStruct((2, 8, lanes), f32),
    ]
    out_specs = [any_spec, any_spec, any_spec]
    if G > 1:
        out_shape.insert(0, jax.ShapeDtypeStruct((G - 1, lines, group, lanes), f32))
        out_specs.insert(0, any_spec)
    *done, raw, lead, pair_out = pl.pallas_call(
        functools.partial(kernel, n, L, R, C, G),
        out_shape=out_shape,
        in_specs=[pl.BlockSpec(memory_space=pltpu.SMEM)] + [hbm] * 8,
        out_specs=out_specs,
        scratch_shapes=[
            *(pltpu.SMEM(a.shape, a.dtype) for a in args[:3]),
            pltpu.VMEM((4, lines, lines), f32),
            pltpu.VMEM((lines, lines), bf16),
            pltpu.VMEM((G, lines, group, lanes), f32),
            pltpu.VMEM((G, lines, group, lanes), f32),
            pltpu.VMEM((L, n, R, lanes), f32),
            pltpu.VMEM((L, half, lanes), f32),
            pltpu.VMEM((L, half, 2 * lanes), f32),
            pltpu.VMEM((L, half, lanes), f32),
            pltpu.VMEM((L, 2 * half, lanes), f32),
            pltpu.VMEM((L, n, R, lanes), f32),
            pltpu.VMEM((max(1, G - 1), lines, group, lanes), f32),
            pltpu.VMEM((5, lines, lines), bf16),
            pltpu.VMEM((5, lines, lines), bf16),
            pltpu.VMEM((2, lines, lines), bf16),
            pltpu.VMEM((2, 8, lanes), f32),
            dma((2,)),
            dma((3,)),
            dma((2,)),
            dma((C,)),
            dma,
            dma,
            dma((C,)),
            dma,
            dma((max(1, C - 1),)),
            dma((G,)),
            dma,
            dma,
            dma,
            dma,
            dma,
            dma((2,)),
        ],
        compiler_params=pltpu.CompilerParams(
            collective_id=0, has_side_effects=True, vmem_limit_bytes=42 << 20
        ),
    )(species, *(pltpu.with_memory_space_constraint(a, pltpu.HBM) for a in (*args, concentration)))

    return pl.pallas_call(
        last_kernel,
        out_shape=whole,
        in_specs=[vmem] * 3 + [any_spec] * len(done),
        out_specs=hbm,
        scratch_shapes=[pltpu.VMEM((lines, group, lanes), f32), dma((G,))],
        compiler_params=pltpu.CompilerParams(vmem_limit_bytes=8 << 20),
    )(lead, pair_out, raw, *done)


def solution(mesh):
    in_specs = (P("groups", "row", "col"), P("groups"), P(), P(), P(), P(), P(), P(), P())
    out_specs = P("groups", "row", "col")
    return jax.shard_map(
        functools.partial(on_device, mesh.shape["row"]),
        mesh=mesh, in_specs=in_specs, out_specs=out_specs, check_vma=False,
    )
```

```python
import functools

import jax
import jax.numpy as jnp
import numpy as np
from jax import lax
from jax.experimental import pallas as pl
from jax.experimental.pallas import tpu as pltpu
from jax.sharding import PartitionSpec as P

MESH = pl.DeviceIdType.MESH
LANES = 128


def react(v, rate, level):
    return v - rate * jnp.tanh(v - level)


def split(v):
    hi = v.astype(jnp.bfloat16)
    lo = (v - hi.astype(jnp.float32)).astype(jnp.bfloat16)
    return hi, lo


def dot3(a, b):
    (ah, al), (bh, bl) = a, b
    dot = functools.partial(jnp.dot, preferred_element_type=jnp.float32)
    return dot(ah, bh) + (dot(ah, bl) + dot(al, bh))


def load_columns(ref, r, width, start, lines):
    rows, lanes = ref.shape[1:]
    if rows % 8 == 0:
        flat = ref.reshape(ref.shape[0] * rows, lanes)
        parts = [flat[pl.ds(start * rows + r + i, lines, stride=rows), :] for i in range(width)]
    else:
        parts = [ref[start : start + lines, r + i, :] for i in range(width)]
    return jnp.concatenate(parts, axis=1)


def store_columns(ref, r, width, value):
    lines, rows, lanes = ref.shape
    for i in range(width):
        part = value[:, i * lanes : (i + 1) * lanes]
        if rows % 8 == 0:
            flat = ref.reshape(lines * rows, lanes)
            flat[pl.ds(r + i, lines, stride=rows), :] = part
        else:
            ref[:, r + i, :] = part


def move(source, target):
    return jnp.dot(source, target, preferred_element_type=jnp.float32).astype(jnp.bfloat16)


def exchange_matrix(size):
    i = lax.broadcasted_iota(jnp.int32, (size, size), 0)
    j = lax.broadcasted_iota(jnp.int32, (size, size), 1)
    return jnp.where(i + j == size - 1, 1.0, 0.0).astype(jnp.bfloat16)


def orientations(matrix, exchange):
    halves = split(matrix)
    return halves, tuple(move(move(exchange, m), exchange) for m in halves)


def choose(flag, plain, turned):
    where = jnp.full(plain[0].shape, flag, jnp.int32) == 1
    return tuple(
        jnp.where(where, b.astype(jnp.float32), a.astype(jnp.float32)).astype(jnp.bfloat16)
        for a, b in zip(plain, turned)
    )


def fold(inverse, explicit, transposed):
    if transposed:
        inverse, explicit = explicit.T, inverse.T
    return dot3(split(inverse), split(explicit))


def sweep_columns(matrix, source, target, rate, level, blocks=None):
    lines, rows, _ = source.shape
    cols = 2 if rows % 2 == 0 else 1
    for r in range(0, rows, cols):
        k = split(react(load_columns(source, r, cols, 0, lines), rate, level))
        out, at = dot3(matrix, k), 0
        for start, count in blocks or [(0, lines)]:
            store_columns(target.at[pl.ds(start, count)], r, cols, out[at : at + count])
            at += count


def picked(matrix, blocks):
    size, wide = matrix[0].shape[0], sum(count for _, count in blocks)
    i = lax.broadcasted_iota(jnp.int32, (size, wide), 0)
    j = lax.broadcasted_iota(jnp.int32, (size, wide), 1)
    at, hit = 0, i < 0
    for start, count in blocks:
        hit = hit | ((j >= at) & (j < at + count) & (i == j + (start - at)))
        at += count
    pick = jnp.where(hit, 1.0, 0.0).astype(jnp.bfloat16)
    hi, lo = (move(m, pick) for m in matrix)
    return jnp.concatenate([hi, hi, lo], axis=1)


def some_lines(matrix, ref, r, cols, blocks, rate, level):
    k = jnp.concatenate(
        [load_columns(ref.at[pl.ds(start, count)], r, cols, 0, count) for start, count in blocks], axis=0
    )
    hi, lo = split(react(k, rate, level))
    return jnp.dot(matrix, jnp.concatenate([hi, lo, hi], axis=0), preferred_element_type=jnp.float32)


def kernel(
    n, L, R, C, G,
    species, rates_hbm, levels_hbm, flags_hbm, e_line_hbm, p_line_hbm, e_depth_hbm, p_depth_hbm, x_hbm,
    *refs,
):
    done, refs = (refs[0], refs[1:]) if G > 1 else (None, refs)
    (
        raw, part, late, pair_out,
        rates, levels, flags, mats, flip,
        x, y, z, w, v, h, t, u, f, mh, ml, lead, soon, scalars,
        x_sem, in_sem, mat_sem, own1, own2, send1, recv1, send2, recv2, recv3, a_send, a_recv, b_send, b_recv, o_sem, pass_sem,
    ) = refs
    me = lax.axis_index("row")
    q = lax.axis_index("col")
    per = L // C
    pair = 2 if per % 2 == 0 else 1
    group = R // G

    barrier = pltpu.get_barrier_semaphore()

    def mat_copies(pair):
        sources = ((p_line_hbm, e_line_hbm), (p_depth_hbm, e_depth_hbm))[pair]
        return [
            pltpu.make_async_copy(source, mats.at[2 * pair + i], mat_sem.at[pair])
            for i, source in enumerate(sources)
        ]

    def mat_wait(pair):
        both = mats.at[pl.ds(2 * pair, 2)]
        pltpu.make_async_copy(both, both, mat_sem.at[pair]).wait()

    def x_copy(g):
        return pltpu.make_async_copy(
            x_hbm.at[:, pl.ds(g * group, group)], x.at[g], x_sem.at[min(g, 1)]
        )

    small = [
        pltpu.make_async_copy(source, target, in_sem.at[i])
        for i, (source, target) in enumerate(
            ((flags_hbm, flags), (rates_hbm, rates), (levels_hbm, levels))
        )
    ]
    for copy in [*mat_copies(0), *small, x_copy(0)]:
        copy.start()

    def greet(j, carry):
        pl.semaphore_signal(
            barrier, inc=1, device_id={"row": lax.rem(me + j, n)}, device_id_type=MESH
        )
        return carry

    lax.fori_loop(n // 2, n, greet, 0, unroll=n <= 8)
    lax.fori_loop(1, n // 2, greet, 0, unroll=n <= 8)
    pl.semaphore_signal(barrier, inc=1, device_id={"col": 1 - q}, device_id_type=MESH)

    flip[...] = exchange_matrix(n * L)

    def keep(slot, flag, plain, turned):
        mh[slot], ml[slot] = choose(flag, plain, turned)

    def around(body):
        def turn(j, carry):
            body(lax.rem(me + j, n))
            return carry

        lax.fori_loop(1, n, turn, 0, unroll=n <= 8)

    def send_rows(c, groups):
        def send_to(d):
            for g in groups:
                pltpu.make_async_remote_copy(
                    src_ref=y.at[g, pl.ds(d * L + c * per, per)],
                    dst_ref=z.at[pl.ds(c * per, per), me, pl.ds(g * group, group)],
                    send_sem=send1,
                    recv_sem=recv1.at[c],
                    device_id={"row": d},
                    device_id_type=MESH,
                ).start()

        around(send_to)

    def rows_of(matrix, blocks):
        if len(blocks) == 1:
            return matrix
        return jnp.concatenate([matrix[start : start + count] for start, count in blocks], axis=0)

    if per % 16 == 0:
        ahead = [(d * L, per) for d in range(n)]
        behind = [(d * L + per, L - per) for d in range(n)]
    else:
        ahead, behind = [(0, n * L)], []

    mat_wait(0)
    for copy in [*(x_copy(g) for g in range(1, G)), *mat_copies(1)]:
        copy.start()
    p, e = split(mats[0]), split(mats[1])
    turned_p = tuple(move(rows_of(flip[...], ahead), m) for m in p)
    turned_e = tuple(move(m, flip[...]) for m in e)
    for copy in small:
        copy.wait()
    kind = species[0]
    rate, level = rates[kind], levels[kind]
    p = choose(flags[0, 0], tuple(rows_of(m, ahead) for m in p), turned_p)
    e = choose(flags[0, 0], e, turned_e)
    first = split(dot3(p, e))
    pltpu.make_async_copy(x.at[0], x.at[0], x_sem.at[0]).wait()
    sweep_columns(first, x.at[0], y.at[0], rate, level, ahead)
    pl.semaphore_wait(barrier, n)
    send_rows(0, (0,))
    lines = orientations(fold(mats[0], mats[1], False), flip[...])
    keep(0, flags[0, 0], *lines)
    if behind:
        first = tuple(rows_of(m[0], behind) for m in (mh, ml))
        sweep_columns(first, x.at[0], y.at[0], rate, level, behind)
    if G > 1:
        rest = x.at[pl.ds(1, G - 1)]
        pltpu.make_async_copy(rest, rest, x_sem.at[1]).wait()
    for g in range(1, G):
        sweep_columns((mh[0], ml[0]), x.at[g], y.at[g], rate, level)
    if G > 1:
        send_rows(0, range(1, G))

    def own_copy(c, g):
        return pltpu.make_async_copy(
            y.at[g, pl.ds(me * L + c * per, per)],
            z.at[pl.ds(c * per, per), me, pl.ds(g * group, group)],
            own1.at[c],
        )

    def send_chunk(c, carry):
        send_rows(c, range(G))
        for g in range(G):
            own_copy(c, g).start()
        return carry

    for g in range(G):
        own_copy(0, g).start()
    lax.fori_loop(1, C, send_chunk, 0)

    mat_wait(1)
    keep(1, flags[0, 1], *lines)
    keep(4, flags[1, 1], *lines)
    final = choose(flags[1, 0], *lines)
    lead[0], lead[1] = final
    before = [(d * L, L - per) for d in range(n)]
    soon[...] = picked(final, before)
    late[...] = picked(final, [(d * L + L - per, per) for d in range(n)])
    scalars[0] = jnp.full(scalars.shape[1:], rate, jnp.float32)
    scalars[1] = jnp.full(scalars.shape[1:], level, jnp.float32)
    passed = pltpu.make_async_copy(scalars, pair_out, pass_sem)
    passed.start()
    depths = orientations(fold(mats[2], mats[3], True), flip[...])
    keep(2, flags[0, 2], *depths)
    keep(3, flags[1, 2], *depths)

    half = n * R // 2
    mine = pl.ds(pl.multiple_of(q * half, half), half)
    theirs = pl.ds(pl.multiple_of((1 - q) * half, half), half)
    lanes_mine = pl.ds(pl.multiple_of(q * LANES, LANES), LANES)
    lanes_theirs = pl.ds(pl.multiple_of((1 - q) * LANES, LANES), LANES)
    peer = {"col": 1 - q}

    def lines_at(c):
        return pl.ds(me * L + c * per, per)

    def own_back(c, g):
        target = f.at[g] if g < G - 1 else raw
        source = u.at[pl.ds(c * per, per), me, pl.ds(g * group, group)]
        return pltpu.make_async_copy(source, target.at[lines_at(c)], own2)

    def chunk(c, carry):
        at = pl.ds(c * per, per)
        arrived = z.at[at, pl.ds(0, n - 1)]
        pltpu.make_async_copy(arrived, arrived, recv1.at[c]).wait()
        own = z.at[at, me]
        pltpu.make_async_copy(own, own, own1.at[c]).wait()

        line = tuple(jnp.concatenate([m[1, mine, :], m[1, theirs, :]], axis=0) for m in (mh, ml))
        for s in range(0, per, pair):
            i = c * per + s
            k = jnp.concatenate([z[i + e].reshape(n * R, LANES) for e in range(pair)], axis=1)
            out = dot3(line, split(react(k, rate, level)))
            for e in range(pair):
                part = out[:, e * LANES : (e + 1) * LANES]
                v[i + e, :, lanes_mine] = part[:half]
                w[i + e] = part[half:]
        to_peer = pltpu.make_async_remote_copy(
            src_ref=w.at[at],
            dst_ref=v.at[at, :, lanes_mine],
            send_sem=a_send,
            recv_sem=a_recv,
            device_id=peer,
            device_id_type=MESH,
        )
        to_peer.start()
        to_peer.wait()

        k = v[at].reshape(per * half, 2 * LANES)
        k = dot3(split(react(k, rate, level)), (mh[2], ml[2]))
        depth = tuple(
            jnp.concatenate([m[3, :, lanes_mine], m[3, :, lanes_theirs]], axis=1) for m in (mh, ml)
        )
        k = dot3(split(react(k, rate, level)), depth)
        t[at, mine, :] = k[:, :LANES].reshape(per, half, LANES)
        h[at] = k[:, LANES:].reshape(per, half, LANES)
        to_peer = pltpu.make_async_remote_copy(
            src_ref=h.at[at],
            dst_ref=t.at[at, mine, :],
            send_sem=b_send,
            recv_sem=b_recv,
            device_id=peer,
            device_id_type=MESH,
        )
        to_peer.start()
        to_peer.wait()

        line = (mh[4], ml[4])
        for s in range(0, per, pair):
            i = c * per + s
            k = jnp.concatenate([t[i + e] for e in range(pair)], axis=1)
            out = dot3(line, split(react(k, rate, level)))
            for e in range(pair):
                u[i + e] = out[:, e * LANES : (e + 1) * LANES].reshape(n, R, LANES)

        def send_back(g, recv, d):
            target = f.at[g] if g < G - 1 else raw
            pltpu.make_async_remote_copy(
                src_ref=u.at[at, d, pl.ds(g * group, group)],
                dst_ref=target.at[lines_at(c)],
                send_sem=send2,
                recv_sem=recv,
                device_id={"row": d},
                device_id_type=MESH,
            ).start()

        @pl.when(c < C - 1)
        def _():
            def send_to(d):
                for g in range(G):
                    send_back(g, recv2.at[c], d)

            around(send_to)

        @pl.when(c == C - 1)
        def _():
            for g in range(G):
                around(functools.partial(send_back, g, recv3.at[g]))

        for g in range(G):
            own_back(c, g).start()
        return carry

    lax.fori_loop(0, C, chunk, 0)
    passed.wait()

    own = z.at[:, me]
    pltpu.make_async_copy(own, own, own2).wait()

    def wait_back(c, carry):
        arrived = z.at[pl.ds(0, per), pl.ds(0, n - 1)]
        pltpu.make_async_copy(arrived, arrived, recv2.at[c]).wait()
        return carry

    lax.fori_loop(0, C - 1, wait_back, 0)

    def done_copy(g):
        return pltpu.make_async_copy(x.at[g], done.at[g], o_sem)

    for g in range(G - 1):
        arrived = raw.at[pl.ds(0, (n - 1) * per)]
        pltpu.make_async_copy(arrived, arrived, recv3.at[g]).wait()
        sweep_columns((lead[0], lead[1]), f.at[g], x.at[g], rate, level)
        done_copy(g).start()
    cols = 2 if group % 2 == 0 else 1
    for r in range(0, group, cols):
        store_columns(part, r, cols, some_lines(soon[...], raw, r, cols, before, rate, level))
    if G > 1:
        pltpu.make_async_copy(done, done, o_sem).wait()
    away = z.at[:, pl.ds(0, n - 1)]
    pltpu.make_async_copy(away, away, send1).wait()
    pltpu.make_async_copy(away, away, send2).wait()
    arrived = raw.at[pl.ds(0, (n - 1) * per)]
    pltpu.make_async_copy(arrived, arrived, recv3.at[G - 1]).wait()


def last_kernel(blocks, late, pair_in, raw, part, *refs):
    *done, o, out, sem = refs
    lines, group, lanes = raw.shape
    G = o.shape[1] // group

    def o_copy(g):
        source = done[0].at[g] if g < G - 1 else out
        return pltpu.make_async_copy(source, o.at[:, pl.ds(g * group, group)], sem.at[g])

    for g in range(G - 1):
        o_copy(g).start()
    cols = 2 if group % 2 == 0 else 1
    rate, level = (jnp.concatenate([pair_in[i, 0:1, :]] * cols, axis=1) for i in range(2))
    for r in range(0, group, cols):
        total = load_columns(part, r, cols, 0, lines)
        total += some_lines(late[...], raw, r, cols, blocks, rate, level)
        store_columns(out, r, cols, total)
    o_copy(G - 1).start()
    for g in range(G):
        o_copy(g).wait()


def on_device(
    n,
    concentration,
    species,
    reaction_rates,
    levels,
    sweep_flags,
    explicit_line,
    inverse_line,
    explicit_depth,
    inverse_depth,
):
    lines, R, lanes = concentration.shape
    L = lines // n
    C = max(2, L // 16)
    G = max(1, R // 8)
    per = L // C
    half = n * R // 2
    group = R // G
    f32, bf16 = jnp.float32, jnp.bfloat16

    any_spec = pl.BlockSpec(memory_space=pl.ANY)
    hbm = pl.BlockSpec(memory_space=pltpu.HBM)
    vmem = pl.BlockSpec(memory_space=pltpu.VMEM)
    dma = pltpu.SemaphoreType.DMA
    whole = jax.ShapeDtypeStruct(concentration.shape, f32)
    args = (
        reaction_rates, levels, sweep_flags,
        explicit_line, inverse_line, explicit_depth, inverse_depth,
    )
    out_shape = [
        jax.ShapeDtypeStruct((lines, group, lanes), f32),
        jax.ShapeDtypeStruct((lines, group, lanes), f32),
        jax.ShapeDtypeStruct((lines, 3 * n * per), bf16),
        jax.ShapeDtypeStruct((2, 8, lanes), f32),
    ]
    out_specs = [vmem, vmem, vmem, any_spec]
    if G > 1:
        out_shape.insert(0, jax.ShapeDtypeStruct((G - 1, lines, group, lanes), f32))
        out_specs.insert(0, any_spec)
    *done, raw, part, late, pair_out = pl.pallas_call(
        functools.partial(kernel, n, L, R, C, G),
        out_shape=out_shape,
        in_specs=[pl.BlockSpec(memory_space=pltpu.SMEM)] + [hbm] * 8,
        out_specs=out_specs,
        scratch_shapes=[
            *(pltpu.SMEM(a.shape, a.dtype) for a in args[:3]),
            pltpu.VMEM((4, lines, lines), f32),
            pltpu.VMEM((lines, lines), bf16),
            pltpu.VMEM((G, lines, group, lanes), f32),
            pltpu.VMEM((G, lines, group, lanes), f32),
            pltpu.VMEM((L, n, R, lanes), f32),
            pltpu.VMEM((L, half, lanes), f32),
            pltpu.VMEM((L, half, 2 * lanes), f32),
            pltpu.VMEM((L, half, lanes), f32),
            pltpu.VMEM((L, 2 * half, lanes), f32),
            pltpu.VMEM((L, n, R, lanes), f32),
            pltpu.VMEM((max(1, G - 1), lines, group, lanes), f32),
            pltpu.VMEM((5, lines, lines), bf16),
            pltpu.VMEM((5, lines, lines), bf16),
            pltpu.VMEM((2, lines, lines), bf16),
            pltpu.VMEM((lines, 3 * (lines - n * per)), bf16),
            pltpu.VMEM((2, 8, lanes), f32),
            dma((2,)),
            dma((3,)),
            dma((2,)),
            dma((C,)),
            dma,
            dma,
            dma((C,)),
            dma,
            dma((max(1, C - 1),)),
            dma((G,)),
            dma,
            dma,
            dma,
            dma,
            dma,
            dma,
        ],
        compiler_params=pltpu.CompilerParams(
            collective_id=0, has_side_effects=True, vmem_limit_bytes=42 << 20
        ),
    )(species, *(pltpu.with_memory_space_constraint(a, pltpu.HBM) for a in (*args, concentration)))

    return pl.pallas_call(
        functools.partial(last_kernel, [(d * L + L - per, per) for d in range(n)]),
        out_shape=whole,
        in_specs=[vmem] * 4 + [any_spec] * len(done),
        out_specs=hbm,
        scratch_shapes=[pltpu.VMEM((lines, group, lanes), f32), dma((G,))],
        compiler_params=pltpu.CompilerParams(vmem_limit_bytes=8 << 20),
    )(late, pair_out, raw, part, *done)


def solution(mesh):
    in_specs = (P("groups", "row", "col"), P("groups"), P(), P(), P(), P(), P(), P(), P())
    out_specs = P("groups", "row", "col")
    return jax.shard_map(
        functools.partial(on_device, mesh.shape["row"]),
        mesh=mesh, in_specs=in_specs, out_specs=out_specs, check_vma=False,
    )
```

```python
import functools

import jax
import jax.numpy as jnp
import numpy as np
from jax import lax
from jax.experimental import pallas as pl
from jax.experimental.pallas import tpu as pltpu
from jax.sharding import PartitionSpec as P

MESH = pl.DeviceIdType.MESH
LANES = 128


def react(v, rate, level):
    return v - rate * jnp.tanh(v - level)


def split(v):
    hi = v.astype(jnp.bfloat16)
    lo = (v - hi.astype(jnp.float32)).astype(jnp.bfloat16)
    return hi, lo


def dot3(a, b):
    (ah, al), (bh, bl) = a, b
    dot = functools.partial(jnp.dot, preferred_element_type=jnp.float32)
    return dot(ah, bh) + (dot(ah, bl) + dot(al, bh))


def load_columns(ref, r, width, start, lines):
    rows, lanes = ref.shape[1:]
    if rows % 8 == 0:
        flat = ref.reshape(ref.shape[0] * rows, lanes)
        parts = [flat[pl.ds(start * rows + r + i, lines, stride=rows), :] for i in range(width)]
    else:
        parts = [ref[start : start + lines, r + i, :] for i in range(width)]
    return jnp.concatenate(parts, axis=1)


def store_columns(ref, r, width, value):
    lines, rows, lanes = ref.shape
    for i in range(width):
        part = value[:, i * lanes : (i + 1) * lanes]
        if rows % 8 == 0:
            flat = ref.reshape(lines * rows, lanes)
            flat[pl.ds(r + i, lines, stride=rows), :] = part
        else:
            ref[:, r + i, :] = part


def move(source, target):
    return jnp.dot(source, target, preferred_element_type=jnp.float32).astype(jnp.bfloat16)


def exchange_matrix(size):
    i = lax.broadcasted_iota(jnp.int32, (size, size), 0)
    j = lax.broadcasted_iota(jnp.int32, (size, size), 1)
    return jnp.where(i + j == size - 1, 1.0, 0.0).astype(jnp.bfloat16)


def orientations(matrix, exchange):
    halves = split(matrix)
    return halves, tuple(move(move(exchange, m), exchange) for m in halves)


def choose(flag, plain, turned):
    where = jnp.full(plain[0].shape, flag, jnp.int32) == 1
    return tuple(
        jnp.where(where, b.astype(jnp.float32), a.astype(jnp.float32)).astype(jnp.bfloat16)
        for a, b in zip(plain, turned)
    )


def fold(inverse, explicit, transposed):
    if transposed:
        inverse, explicit = explicit.T, inverse.T
    return dot3(split(inverse), split(explicit))


def sweep_columns(matrix, source, target, rate, level, blocks=None):
    lines, rows, _ = source.shape
    cols = 2 if rows % 2 == 0 else 1
    for r in range(0, rows, cols):
        k = split(react(load_columns(source, r, cols, 0, lines), rate, level))
        out, at = dot3(matrix, k), 0
        for start, count in blocks or [(0, lines)]:
            store_columns(target.at[pl.ds(start, count)], r, cols, out[at : at + count])
            at += count


def picked(matrix, blocks):
    size, wide = matrix[0].shape[0], sum(count for _, count in blocks)
    i = lax.broadcasted_iota(jnp.int32, (size, wide), 0)
    j = lax.broadcasted_iota(jnp.int32, (size, wide), 1)
    at, hit = 0, i < 0
    for start, count in blocks:
        hit = hit | ((j >= at) & (j < at + count) & (i == j + (start - at)))
        at += count
    pick = jnp.where(hit, 1.0, 0.0).astype(jnp.bfloat16)
    hi, lo = (move(m, pick) for m in matrix)
    return jnp.concatenate([hi, hi, lo], axis=1)


def some_lines(matrix, ref, r, cols, blocks, rate, level):
    k = jnp.concatenate(
        [load_columns(ref.at[pl.ds(start, count)], r, cols, 0, count) for start, count in blocks], axis=0
    )
    hi, lo = split(react(k, rate, level))
    return jnp.dot(matrix, jnp.concatenate([hi, lo, hi], axis=0), preferred_element_type=jnp.float32)


def kernel(
    n, L, R, C, G,
    species, rates_hbm, levels_hbm, flags_hbm, e_line_hbm, p_line_hbm, e_depth_hbm, p_depth_hbm, x_hbm,
    *refs,
):
    done, refs = (refs[0], refs[1:]) if G > 1 else (None, refs)
    (
        raw, part, late, pair_out,
        rates, levels, flags, mats, flip,
        x, y, z, w, v, h, t, u, f, mh, ml, lead, soon, scalars,
        x_sem, in_sem, mat_sem, own1, own2, send1, recv1, send2, recv2, recv3, a_send, a_recv, b_send, b_recv, o_sem, pass_sem,
    ) = refs
    me = lax.axis_index("row")
    q = lax.axis_index("col")
    per = L // C
    pair = 2 if per % 2 == 0 else 1
    group = R // G

    barrier = pltpu.get_barrier_semaphore()

    def mat_copies(pair):
        sources = ((p_line_hbm, e_line_hbm), (p_depth_hbm, e_depth_hbm))[pair]
        return [
            pltpu.make_async_copy(source, mats.at[2 * pair + i], mat_sem.at[pair])
            for i, source in enumerate(sources)
        ]

    def mat_wait(pair):
        both = mats.at[pl.ds(2 * pair, 2)]
        pltpu.make_async_copy(both, both, mat_sem.at[pair]).wait()

    def x_copy(g):
        return pltpu.make_async_copy(
            x_hbm.at[:, pl.ds(g * group, group)], x.at[g], x_sem.at[min(g, 1)]
        )

    small = [
        pltpu.make_async_copy(source, target, in_sem.at[i])
        for i, (source, target) in enumerate(
            ((flags_hbm, flags), (rates_hbm, rates), (levels_hbm, levels))
        )
    ]
    for copy in [*mat_copies(0), *small, x_copy(0)]:
        copy.start()

    def greet(j, carry):
        pl.semaphore_signal(
            barrier, inc=1, device_id={"row": lax.rem(me + j, n)}, device_id_type=MESH
        )
        return carry

    lax.fori_loop(n // 2, n, greet, 0, unroll=n <= 8)
    lax.fori_loop(1, n // 2, greet, 0, unroll=n <= 8)
    pl.semaphore_signal(barrier, inc=1, device_id={"col": 1 - q}, device_id_type=MESH)

    flip[...] = exchange_matrix(n * L)

    def keep(slot, flag, plain, turned):
        mh[slot], ml[slot] = choose(flag, plain, turned)

    def around(body):
        def turn(j, carry):
            body(lax.rem(me + j, n))
            return carry

        lax.fori_loop(1, n, turn, 0, unroll=n <= 8)

    def send_rows(c, groups):
        def send_to(d):
            for g in groups:
                pltpu.make_async_remote_copy(
                    src_ref=y.at[g, pl.ds(d * L + c * per, per)],
                    dst_ref=z.at[pl.ds(c * per, per), me, pl.ds(g * group, group)],
                    send_sem=send1,
                    recv_sem=recv1.at[c],
                    device_id={"row": d},
                    device_id_type=MESH,
                ).start()

        around(send_to)

    def rows_of(matrix, blocks):
        if len(blocks) == 1:
            return matrix
        return jnp.concatenate([matrix[start : start + count] for start, count in blocks], axis=0)

    if per % 16 == 0:
        ahead = [(d * L, per) for d in range(n)]
        behind = [(d * L + per, L - per) for d in range(n)]
    else:
        ahead, behind = [(0, n * L)], []

    mat_wait(0)
    for copy in [*(x_copy(g) for g in range(1, G)), *mat_copies(1)]:
        copy.start()
    p, e = split(mats[0]), split(mats[1])
    turned_p = tuple(move(rows_of(flip[...], ahead), m) for m in p)
    turned_e = tuple(move(m, flip[...]) for m in e)
    for copy in small:
        copy.wait()
    pltpu.make_async_copy(x.at[0], x.at[0], x_sem.at[0]).wait()
    kind = species[0]
    rate, level = rates[kind], levels[kind]
    p = choose(flags[0, 0], tuple(rows_of(m, ahead) for m in p), turned_p)
    e = choose(flags[0, 0], e, turned_e)
    first = split(dot3(p, e))
    sweep_columns(first, x.at[0], y.at[0], rate, level, ahead)
    pl.semaphore_wait(barrier, n)
    send_rows(0, (0,))
    lines = orientations(fold(mats[0], mats[1], False), flip[...])
    keep(0, flags[0, 0], *lines)
    if behind:
        first = tuple(rows_of(m[0], behind) for m in (mh, ml))
        sweep_columns(first, x.at[0], y.at[0], rate, level, behind)
    if G > 1:
        rest = x.at[pl.ds(1, G - 1)]
        pltpu.make_async_copy(rest, rest, x_sem.at[1]).wait()
    for g in range(1, G):
        sweep_columns((mh[0], ml[0]), x.at[g], y.at[g], rate, level)
    if G > 1:
        send_rows(0, range(1, G))

    def own_copy(c, g):
        return pltpu.make_async_copy(
            y.at[g, pl.ds(me * L + c * per, per)],
            z.at[pl.ds(c * per, per), me, pl.ds(g * group, group)],
            own1.at[c],
        )

    def send_chunk(c, carry):
        send_rows(c, range(G))
        for g in range(G):
            own_copy(c, g).start()
        return carry

    for g in range(G):
        own_copy(0, g).start()
    lax.fori_loop(1, C, send_chunk, 0)

    mat_wait(1)
    keep(1, flags[0, 1], *lines)
    keep(4, flags[1, 1], *lines)
    final = choose(flags[1, 0], *lines)
    lead[0], lead[1] = final
    before = [(d * L, L - per) for d in range(n)]
    soon[...] = picked(final, before)
    late[...] = picked(final, [(d * L + L - per, per) for d in range(n)])
    scalars[0] = jnp.full(scalars.shape[1:], rate, jnp.float32)
    scalars[1] = jnp.full(scalars.shape[1:], level, jnp.float32)
    passed = pltpu.make_async_copy(scalars, pair_out, pass_sem)
    passed.start()
    depths = orientations(fold(mats[2], mats[3], True), flip[...])
    keep(2, flags[0, 2], *depths)
    keep(3, flags[1, 2], *depths)

    half = n * R // 2
    mine = pl.ds(pl.multiple_of(q * half, half), half)
    theirs = pl.ds(pl.multiple_of((1 - q) * half, half), half)
    lanes_mine = pl.ds(pl.multiple_of(q * LANES, LANES), LANES)
    lanes_theirs = pl.ds(pl.multiple_of((1 - q) * LANES, LANES), LANES)
    peer = {"col": 1 - q}

    def lines_at(c):
        return pl.ds(me * L + c * per, per)

    def own_back(c, g):
        target = f.at[g] if g < G - 1 else raw
        source = u.at[pl.ds(c * per, per), me, pl.ds(g * group, group)]
        return pltpu.make_async_copy(source, target.at[lines_at(c)], own2)

    def chunk(c, carry):
        at = pl.ds(c * per, per)
        arrived = z.at[at, pl.ds(0, n - 1)]
        pltpu.make_async_copy(arrived, arrived, recv1.at[c]).wait()
        own = z.at[at, me]
        pltpu.make_async_copy(own, own, own1.at[c]).wait()

        line = tuple(jnp.concatenate([m[1, mine, :], m[1, theirs, :]], axis=0) for m in (mh, ml))
        for s in range(0, per, pair):
            i = c * per + s
            k = jnp.concatenate([z[i + e].reshape(n * R, LANES) for e in range(pair)], axis=1)
            out = dot3(line, split(react(k, rate, level)))
            for e in range(pair):
                part = out[:, e * LANES : (e + 1) * LANES]
                v[i + e, :, lanes_mine] = part[:half]
                w[i + e] = part[half:]
        to_peer = pltpu.make_async_remote_copy(
            src_ref=w.at[at],
            dst_ref=v.at[at, :, lanes_mine],
            send_sem=a_send,
            recv_sem=a_recv,
            device_id=peer,
            device_id_type=MESH,
        )
        to_peer.start()
        to_peer.wait()

        k = v[at].reshape(per * half, 2 * LANES)
        k = dot3(split(react(k, rate, level)), (mh[2], ml[2]))
        depth = tuple(
            jnp.concatenate([m[3, :, lanes_mine], m[3, :, lanes_theirs]], axis=1) for m in (mh, ml)
        )
        k = dot3(split(react(k, rate, level)), depth)
        t[at, mine, :] = k[:, :LANES].reshape(per, half, LANES)
        h[at] = k[:, LANES:].reshape(per, half, LANES)
        to_peer = pltpu.make_async_remote_copy(
            src_ref=h.at[at],
            dst_ref=t.at[at, mine, :],
            send_sem=b_send,
            recv_sem=b_recv,
            device_id=peer,
            device_id_type=MESH,
        )
        to_peer.start()
        to_peer.wait()

        line = (mh[4], ml[4])
        for s in range(0, per, pair):
            i = c * per + s
            k = jnp.concatenate([t[i + e] for e in range(pair)], axis=1)
            out = dot3(line, split(react(k, rate, level)))
            for e in range(pair):
                u[i + e] = out[:, e * LANES : (e + 1) * LANES].reshape(n, R, LANES)

        def send_back(g, recv, d):
            target = f.at[g] if g < G - 1 else raw
            pltpu.make_async_remote_copy(
                src_ref=u.at[at, d, pl.ds(g * group, group)],
                dst_ref=target.at[lines_at(c)],
                send_sem=send2,
                recv_sem=recv,
                device_id={"row": d},
                device_id_type=MESH,
            ).start()

        @pl.when(c < C - 1)
        def _():
            def send_to(d):
                for g in range(G):
                    send_back(g, recv2.at[c], d)

            around(send_to)

        @pl.when(c == C - 1)
        def _():
            for g in range(G):
                around(functools.partial(send_back, g, recv3.at[g]))

        for g in range(G):
            own_back(c, g).start()
        return carry

    lax.fori_loop(0, C, chunk, 0)
    passed.wait()

    own = z.at[:, me]
    pltpu.make_async_copy(own, own, own2).wait()

    def wait_back(c, carry):
        arrived = z.at[pl.ds(0, per), pl.ds(0, n - 1)]
        pltpu.make_async_copy(arrived, arrived, recv2.at[c]).wait()
        return carry

    lax.fori_loop(0, C - 1, wait_back, 0)

    def done_copy(g):
        return pltpu.make_async_copy(x.at[g], done.at[g], o_sem)

    for g in range(G - 1):
        arrived = raw.at[pl.ds(0, (n - 1) * per)]
        pltpu.make_async_copy(arrived, arrived, recv3.at[g]).wait()
        sweep_columns((lead[0], lead[1]), f.at[g], x.at[g], rate, level)
        done_copy(g).start()
    cols = 2 if group % 2 == 0 else 1
    for r in range(0, group, cols):
        store_columns(part, r, cols, some_lines(soon[...], raw, r, cols, before, rate, level))
    if G > 1:
        pltpu.make_async_copy(done, done, o_sem).wait()
    away = z.at[:, pl.ds(0, n - 1)]
    pltpu.make_async_copy(away, away, send1).wait()
    pltpu.make_async_copy(away, away, send2).wait()
    arrived = raw.at[pl.ds(0, (n - 1) * per)]
    pltpu.make_async_copy(arrived, arrived, recv3.at[G - 1]).wait()


def last_kernel(blocks, late, pair_in, raw, part, *refs):
    *done, o, out, sem = refs
    lines, group, lanes = raw.shape
    G = o.shape[1] // group

    def o_copy(g):
        source = done[0].at[g] if g < G - 1 else out
        return pltpu.make_async_copy(source, o.at[:, pl.ds(g * group, group)], sem.at[g])

    for g in range(G - 1):
        o_copy(g).start()
    cols = 2 if group % 2 == 0 else 1
    rate, level = (jnp.concatenate([pair_in[i, 0:1, :]] * cols, axis=1) for i in range(2))
    for r in range(0, group, cols):
        total = load_columns(part, r, cols, 0, lines)
        total += some_lines(late[...], raw, r, cols, blocks, rate, level)
        store_columns(out, r, cols, total)
    o_copy(G - 1).start()
    for g in range(G):
        o_copy(g).wait()


def on_device(
    n,
    concentration,
    species,
    reaction_rates,
    levels,
    sweep_flags,
    explicit_line,
    inverse_line,
    explicit_depth,
    inverse_depth,
):
    lines, R, lanes = concentration.shape
    L = lines // n
    C = max(2, L // 16)
    G = max(1, R // 8)
    per = L // C
    half = n * R // 2
    group = R // G
    f32, bf16 = jnp.float32, jnp.bfloat16

    any_spec = pl.BlockSpec(memory_space=pl.ANY)
    hbm = pl.BlockSpec(memory_space=pltpu.HBM)
    vmem = pl.BlockSpec(memory_space=pltpu.VMEM)
    dma = pltpu.SemaphoreType.DMA
    whole = jax.ShapeDtypeStruct(concentration.shape, f32)
    args = (
        reaction_rates, levels, sweep_flags,
        explicit_line, inverse_line, explicit_depth, inverse_depth,
    )
    out_shape = [
        jax.ShapeDtypeStruct((lines, group, lanes), f32),
        jax.ShapeDtypeStruct((lines, group, lanes), f32),
        jax.ShapeDtypeStruct((lines, 3 * n * per), bf16),
        jax.ShapeDtypeStruct((2, 8, lanes), f32),
    ]
    out_specs = [vmem, vmem, vmem, any_spec]
    if G > 1:
        out_shape.insert(0, jax.ShapeDtypeStruct((G - 1, lines, group, lanes), f32))
        out_specs.insert(0, any_spec)
    *done, raw, part, late, pair_out = pl.pallas_call(
        functools.partial(kernel, n, L, R, C, G),
        out_shape=out_shape,
        in_specs=[pl.BlockSpec(memory_space=pltpu.SMEM)] + [hbm] * 8,
        out_specs=out_specs,
        scratch_shapes=[
            *(pltpu.SMEM(a.shape, a.dtype) for a in args[:3]),
            pltpu.VMEM((4, lines, lines), f32),
            pltpu.VMEM((lines, lines), bf16),
            pltpu.VMEM((G, lines, group, lanes), f32),
            pltpu.VMEM((G, lines, group, lanes), f32),
            pltpu.VMEM((L, n, R, lanes), f32),
            pltpu.VMEM((L, half, lanes), f32),
            pltpu.VMEM((L, half, 2 * lanes), f32),
            pltpu.VMEM((L, half, lanes), f32),
            pltpu.VMEM((L, 2 * half, lanes), f32),
            pltpu.VMEM((L, n, R, lanes), f32),
            pltpu.VMEM((max(1, G - 1), lines, group, lanes), f32),
            pltpu.VMEM((5, lines, lines), bf16),
            pltpu.VMEM((5, lines, lines), bf16),
            pltpu.VMEM((2, lines, lines), bf16),
            pltpu.VMEM((lines, 3 * (lines - n * per)), bf16),
            pltpu.VMEM((2, 8, lanes), f32),
            dma((2,)),
            dma((3,)),
            dma((2,)),
            dma((C,)),
            dma,
            dma,
            dma((C,)),
            dma,
            dma((max(1, C - 1),)),
            dma((G,)),
            dma,
            dma,
            dma,
            dma,
            dma,
            dma,
        ],
        compiler_params=pltpu.CompilerParams(
            collective_id=0, has_side_effects=True, vmem_limit_bytes=42 << 20
        ),
    )(species, *(pltpu.with_memory_space_constraint(a, pltpu.HBM) for a in (*args, concentration)))

    return pl.pallas_call(
        functools.partial(last_kernel, [(d * L + L - per, per) for d in range(n)]),
        out_shape=whole,
        in_specs=[vmem] * 4 + [any_spec] * len(done),
        out_specs=hbm,
        scratch_shapes=[pltpu.VMEM((lines, group, lanes), f32), dma((G,))],
        compiler_params=pltpu.CompilerParams(vmem_limit_bytes=8 << 20),
    )(late, pair_out, raw, part, *done)


def solution(mesh):
    in_specs = (P("groups", "row", "col"), P("groups"), P(), P(), P(), P(), P(), P(), P())
    out_specs = P("groups", "row", "col")
    return jax.shard_map(
        functools.partial(on_device, mesh.shape["row"]),
        mesh=mesh, in_specs=in_specs, out_specs=out_specs, check_vma=False,
    )
```

```python
import functools

import jax
import jax.numpy as jnp
import numpy as np
from jax import lax
from jax.experimental import pallas as pl
from jax.experimental.pallas import tpu as pltpu
from jax.sharding import PartitionSpec as P

MESH = pl.DeviceIdType.MESH
LANES = 128


def react(v, rate, level):
    return v - rate * jnp.tanh(v - level)


def split(v):
    hi = v.astype(jnp.bfloat16)
    lo = (v - hi.astype(jnp.float32)).astype(jnp.bfloat16)
    return hi, lo


def dot3(a, b):
    (ah, al), (bh, bl) = a, b
    dot = functools.partial(jnp.dot, preferred_element_type=jnp.float32)
    return dot(ah, bh) + (dot(ah, bl) + dot(al, bh))


def load_columns(ref, r, width, start, lines):
    rows, lanes = ref.shape[1:]
    if rows % 8 == 0:
        flat = ref.reshape(ref.shape[0] * rows, lanes)
        parts = [flat[pl.ds(start * rows + r + i, lines, stride=rows), :] for i in range(width)]
    else:
        parts = [ref[start : start + lines, r + i, :] for i in range(width)]
    return jnp.concatenate(parts, axis=1)


def store_columns(ref, r, width, value):
    lines, rows, lanes = ref.shape
    for i in range(width):
        part = value[:, i * lanes : (i + 1) * lanes]
        if rows % 8 == 0:
            flat = ref.reshape(lines * rows, lanes)
            flat[pl.ds(r + i, lines, stride=rows), :] = part
        else:
            ref[:, r + i, :] = part


def move(source, target):
    return jnp.dot(source, target, preferred_element_type=jnp.float32).astype(jnp.bfloat16)


def exchange_matrix(size):
    i = lax.broadcasted_iota(jnp.int32, (size, size), 0)
    j = lax.broadcasted_iota(jnp.int32, (size, size), 1)
    return jnp.where(i + j == size - 1, 1.0, 0.0).astype(jnp.bfloat16)


def orientations(matrix, exchange):
    halves = split(matrix)
    return halves, tuple(move(move(exchange, m), exchange) for m in halves)


def choose(flag, plain, turned):
    where = jnp.full(plain[0].shape, flag, jnp.int32) == 1
    return tuple(
        jnp.where(where, b.astype(jnp.float32), a.astype(jnp.float32)).astype(jnp.bfloat16)
        for a, b in zip(plain, turned)
    )


def fold(inverse, explicit, transposed):
    if transposed:
        inverse, explicit = explicit.T, inverse.T
    return dot3(split(inverse), split(explicit))


def sweep_columns(matrix, source, target, rate, level, blocks=None):
    lines, rows, _ = source.shape
    cols = 2 if rows % 2 == 0 else 1
    for r in range(0, rows, cols):
        k = split(react(load_columns(source, r, cols, 0, lines), rate, level))
        out, at = dot3(matrix, k), 0
        for start, count in blocks or [(0, lines)]:
            store_columns(target.at[pl.ds(start, count)], r, cols, out[at : at + count])
            at += count


def picked(matrix, blocks):
    size, wide = matrix[0].shape[0], sum(count for _, count in blocks)
    i = lax.broadcasted_iota(jnp.int32, (size, wide), 0)
    j = lax.broadcasted_iota(jnp.int32, (size, wide), 1)
    at, hit = 0, i < 0
    for start, count in blocks:
        hit = hit | ((j >= at) & (j < at + count) & (i == j + (start - at)))
        at += count
    pick = jnp.where(hit, 1.0, 0.0).astype(jnp.bfloat16)
    hi, lo = (move(m, pick) for m in matrix)
    return jnp.concatenate([hi, hi, lo], axis=1)


def some_lines(matrix, ref, r, cols, blocks, rate, level):
    k = jnp.concatenate(
        [load_columns(ref.at[pl.ds(start, count)], r, cols, 0, count) for start, count in blocks], axis=0
    )
    hi, lo = split(react(k, rate, level))
    return jnp.dot(matrix, jnp.concatenate([hi, lo, hi], axis=0), preferred_element_type=jnp.float32)


def kernel(
    n, L, R, C, G,
    species, rates_hbm, levels_hbm, flags_hbm, e_line_hbm, p_line_hbm, e_depth_hbm, p_depth_hbm, x_hbm,
    *refs,
):
    done, refs = (refs[0], refs[1:]) if G > 1 else (None, refs)
    (
        raw, part, late, pair_out,
        rates, levels, flags, mats, flip,
        x, y, z, w, v, h, t, u, f, mh, ml, lead, soon, scalars,
        x_sem, in_sem, mat_sem, own1, own2, send1, recv1, send2, recv2, recv3, a_send, a_recv, b_send, b_recv, o_sem, pass_sem,
    ) = refs
    me = lax.axis_index("row")
    q = lax.axis_index("col")
    per = L // C
    pair = 2 if per % 2 == 0 else 1
    group = R // G

    barrier = pltpu.get_barrier_semaphore()

    def mat_copies(pair):
        sources = ((p_line_hbm, e_line_hbm), (p_depth_hbm, e_depth_hbm))[pair]
        return [
            pltpu.make_async_copy(source, mats.at[2 * pair + i], mat_sem.at[pair])
            for i, source in enumerate(sources)
        ]

    def mat_wait(pair):
        both = mats.at[pl.ds(2 * pair, 2)]
        pltpu.make_async_copy(both, both, mat_sem.at[pair]).wait()

    def x_copy(g):
        return pltpu.make_async_copy(
            x_hbm.at[:, pl.ds(g * group, group)], x.at[g], x_sem.at[min(g, 1)]
        )

    small = [
        pltpu.make_async_copy(source, target, in_sem.at[i])
        for i, (source, target) in enumerate(
            ((flags_hbm, flags), (rates_hbm, rates), (levels_hbm, levels))
        )
    ]
    for copy in [*mat_copies(0), *small, x_copy(0)]:
        copy.start()

    def greet(j, carry):
        pl.semaphore_signal(
            barrier, inc=1, device_id={"row": lax.rem(me + j, n)}, device_id_type=MESH
        )
        return carry

    lax.fori_loop(n // 2, n, greet, 0, unroll=n <= 8)
    lax.fori_loop(1, n // 2, greet, 0, unroll=n <= 8)
    pl.semaphore_signal(barrier, inc=1, device_id={"col": 1 - q}, device_id_type=MESH)

    flip[...] = exchange_matrix(n * L)

    def keep(slot, flag, plain, turned):
        mh[slot], ml[slot] = choose(flag, plain, turned)

    def around(body):
        def turn(j, carry):
            body(lax.rem(me + j, n))
            return carry

        lax.fori_loop(1, n, turn, 0, unroll=n <= 8)

    def across_first(body):
        half = n // 2
        other = half - half * (me // half) if n % 2 == 0 else 0

        def across(j, carry):
            body(other + lax.rem(me + j, half))
            return carry

        def beside(j, carry):
            body(half - other + lax.rem(me + j, half))
            return carry

        lax.fori_loop(0, half, across, 0, unroll=n <= 8)
        lax.fori_loop(1, half, beside, 0, unroll=n <= 8)

    def send_rows(c, groups, order=around):
        def send_to(d):
            for g in groups:
                pltpu.make_async_remote_copy(
                    src_ref=y.at[g, pl.ds(d * L + c * per, per)],
                    dst_ref=z.at[pl.ds(c * per, per), me, pl.ds(g * group, group)],
                    send_sem=send1,
                    recv_sem=recv1.at[c],
                    device_id={"row": d},
                    device_id_type=MESH,
                ).start()

        order(send_to)

    def rows_of(matrix, blocks):
        if len(blocks) == 1:
            return matrix
        return jnp.concatenate([matrix[start : start + count] for start, count in blocks], axis=0)

    if per % 16 == 0:
        ahead = [(d * L, per) for d in range(n)]
        behind = [(d * L + per, L - per) for d in range(n)]
    else:
        ahead, behind = [(0, n * L)], []

    mat_wait(0)
    for copy in [*(x_copy(g) for g in range(1, G)), *mat_copies(1)]:
        copy.start()
    p, e = split(mats[0]), split(mats[1])
    turned_p = tuple(move(rows_of(flip[...], ahead), m) for m in p)
    turned_e = tuple(move(m, flip[...]) for m in e)
    for copy in small:
        copy.wait()
    pltpu.make_async_copy(x.at[0], x.at[0], x_sem.at[0]).wait()
    kind = species[0]
    rate, level = rates[kind], levels[kind]
    p = choose(flags[0, 0], tuple(rows_of(m, ahead) for m in p), turned_p)
    e = choose(flags[0, 0], e, turned_e)
    first = split(dot3(p, e))
    sweep_columns(first, x.at[0], y.at[0], rate, level, ahead)
    pl.semaphore_wait(barrier, n)
    send_rows(0, (0,), across_first if n % 2 == 0 else around)
    lines = orientations(fold(mats[0], mats[1], False), flip[...])
    keep(0, flags[0, 0], *lines)
    if behind:
        first = tuple(rows_of(m[0], behind) for m in (mh, ml))
        sweep_columns(first, x.at[0], y.at[0], rate, level, behind)
    if G > 1:
        rest = x.at[pl.ds(1, G - 1)]
        pltpu.make_async_copy(rest, rest, x_sem.at[1]).wait()
    for g in range(1, G):
        sweep_columns((mh[0], ml[0]), x.at[g], y.at[g], rate, level)
    if G > 1:
        send_rows(0, range(1, G))

    def own_copy(c, g):
        return pltpu.make_async_copy(
            y.at[g, pl.ds(me * L + c * per, per)],
            z.at[pl.ds(c * per, per), me, pl.ds(g * group, group)],
            own1.at[c],
        )

    def send_chunk(c, carry):
        send_rows(c, range(G))
        for g in range(G):
            own_copy(c, g).start()
        return carry

    for g in range(G):
        own_copy(0, g).start()
    lax.fori_loop(1, C, send_chunk, 0)

    mat_wait(1)
    keep(1, flags[0, 1], *lines)
    keep(4, flags[1, 1], *lines)
    final = choose(flags[1, 0], *lines)
    lead[0], lead[1] = final
    before = [(d * L, L - per) for d in range(n)]
    soon[...] = picked(final, before)
    late[...] = picked(final, [(d * L + L - per, per) for d in range(n)])
    scalars[0] = jnp.full(scalars.shape[1:], rate, jnp.float32)
    scalars[1] = jnp.full(scalars.shape[1:], level, jnp.float32)
    passed = pltpu.make_async_copy(scalars, pair_out, pass_sem)
    passed.start()
    depths = orientations(fold(mats[2], mats[3], True), flip[...])
    keep(2, flags[0, 2], *depths)
    keep(3, flags[1, 2], *depths)

    half = n * R // 2
    mine = pl.ds(pl.multiple_of(q * half, half), half)
    theirs = pl.ds(pl.multiple_of((1 - q) * half, half), half)
    lanes_mine = pl.ds(pl.multiple_of(q * LANES, LANES), LANES)
    lanes_theirs = pl.ds(pl.multiple_of((1 - q) * LANES, LANES), LANES)
    peer = {"col": 1 - q}

    def lines_at(c):
        return pl.ds(me * L + c * per, per)

    def own_back(c, g):
        target = f.at[g] if g < G - 1 else raw
        source = u.at[pl.ds(c * per, per), me, pl.ds(g * group, group)]
        return pltpu.make_async_copy(source, target.at[lines_at(c)], own2)

    def chunk(c, carry):
        at = pl.ds(c * per, per)
        arrived = z.at[at, pl.ds(0, n - 1)]
        pltpu.make_async_copy(arrived, arrived, recv1.at[c]).wait()
        own = z.at[at, me]
        pltpu.make_async_copy(own, own, own1.at[c]).wait()

        line = tuple(jnp.concatenate([m[1, mine, :], m[1, theirs, :]], axis=0) for m in (mh, ml))
        for s in range(0, per, pair):
            i = c * per + s
            k = jnp.concatenate([z[i + e].reshape(n * R, LANES) for e in range(pair)], axis=1)
            out = dot3(line, split(react(k, rate, level)))
            for e in range(pair):
                part = out[:, e * LANES : (e + 1) * LANES]
                v[i + e, :, lanes_mine] = part[:half]
                w[i + e] = part[half:]
        to_peer = pltpu.make_async_remote_copy(
            src_ref=w.at[at],
            dst_ref=v.at[at, :, lanes_mine],
            send_sem=a_send,
            recv_sem=a_recv,
            device_id=peer,
            device_id_type=MESH,
        )
        to_peer.start()
        to_peer.wait()

        k = v[at].reshape(per * half, 2 * LANES)
        k = dot3(split(react(k, rate, level)), (mh[2], ml[2]))
        depth = tuple(
            jnp.concatenate([m[3, :, lanes_mine], m[3, :, lanes_theirs]], axis=1) for m in (mh, ml)
        )
        k = dot3(split(react(k, rate, level)), depth)
        t[at, mine, :] = k[:, :LANES].reshape(per, half, LANES)
        h[at] = k[:, LANES:].reshape(per, half, LANES)
        to_peer = pltpu.make_async_remote_copy(
            src_ref=h.at[at],
            dst_ref=t.at[at, mine, :],
            send_sem=b_send,
            recv_sem=b_recv,
            device_id=peer,
            device_id_type=MESH,
        )
        to_peer.start()
        to_peer.wait()

        line = (mh[4], ml[4])
        for s in range(0, per, pair):
            i = c * per + s
            k = jnp.concatenate([t[i + e] for e in range(pair)], axis=1)
            out = dot3(line, split(react(k, rate, level)))
            for e in range(pair):
                u[i + e] = out[:, e * LANES : (e + 1) * LANES].reshape(n, R, LANES)

        def send_back(g, recv, d):
            target = f.at[g] if g < G - 1 else raw
            pltpu.make_async_remote_copy(
                src_ref=u.at[at, d, pl.ds(g * group, group)],
                dst_ref=target.at[lines_at(c)],
                send_sem=send2,
                recv_sem=recv,
                device_id={"row": d},
                device_id_type=MESH,
            ).start()

        @pl.when(c < C - 1)
        def _():
            def send_to(d):
                for g in range(G):
                    send_back(g, recv2.at[c], d)

            around(send_to)

        @pl.when(c == C - 1)
        def _():
            for g in range(G):
                around(functools.partial(send_back, g, recv3.at[g]))

        for g in range(G):
            own_back(c, g).start()
        return carry

    lax.fori_loop(0, C, chunk, 0)
    passed.wait()

    own = z.at[:, me]
    pltpu.make_async_copy(own, own, own2).wait()

    def wait_back(c, carry):
        arrived = z.at[pl.ds(0, per), pl.ds(0, n - 1)]
        pltpu.make_async_copy(arrived, arrived, recv2.at[c]).wait()
        return carry

    lax.fori_loop(0, C - 1, wait_back, 0)

    def done_copy(g):
        return pltpu.make_async_copy(x.at[g], done.at[g], o_sem)

    for g in range(G - 1):
        arrived = raw.at[pl.ds(0, (n - 1) * per)]
        pltpu.make_async_copy(arrived, arrived, recv3.at[g]).wait()
        sweep_columns((lead[0], lead[1]), f.at[g], x.at[g], rate, level)
        done_copy(g).start()
    cols = 2 if group % 2 == 0 else 1
    for r in range(0, group, cols):
        store_columns(part, r, cols, some_lines(soon[...], raw, r, cols, before, rate, level))
    if G > 1:
        pltpu.make_async_copy(done, done, o_sem).wait()
    away = z.at[:, pl.ds(0, n - 1)]
    pltpu.make_async_copy(away, away, send1).wait()
    pltpu.make_async_copy(away, away, send2).wait()
    arrived = raw.at[pl.ds(0, (n - 1) * per)]
    pltpu.make_async_copy(arrived, arrived, recv3.at[G - 1]).wait()


def last_kernel(blocks, late, pair_in, raw, part, *refs):
    *done, o, out, sem = refs
    lines, group, lanes = raw.shape
    G = o.shape[1] // group

    def o_copy(g):
        source = done[0].at[g] if g < G - 1 else out
        return pltpu.make_async_copy(source, o.at[:, pl.ds(g * group, group)], sem.at[g])

    for g in range(G - 1):
        o_copy(g).start()
    cols = 2 if group % 2 == 0 else 1
    rate, level = (jnp.concatenate([pair_in[i, 0:1, :]] * cols, axis=1) for i in range(2))
    for r in range(0, group, cols):
        total = load_columns(part, r, cols, 0, lines)
        total += some_lines(late[...], raw, r, cols, blocks, rate, level)
        store_columns(out, r, cols, total)
    o_copy(G - 1).start()
    for g in range(G):
        o_copy(g).wait()


def on_device(
    n,
    concentration,
    species,
    reaction_rates,
    levels,
    sweep_flags,
    explicit_line,
    inverse_line,
    explicit_depth,
    inverse_depth,
):
    lines, R, lanes = concentration.shape
    L = lines // n
    C = max(2, L // 16)
    G = max(1, R // 8)
    per = L // C
    half = n * R // 2
    group = R // G
    f32, bf16 = jnp.float32, jnp.bfloat16

    any_spec = pl.BlockSpec(memory_space=pl.ANY)
    hbm = pl.BlockSpec(memory_space=pltpu.HBM)
    vmem = pl.BlockSpec(memory_space=pltpu.VMEM)
    dma = pltpu.SemaphoreType.DMA
    whole = jax.ShapeDtypeStruct(concentration.shape, f32)
    args = (
        reaction_rates, levels, sweep_flags,
        explicit_line, inverse_line, explicit_depth, inverse_depth,
    )
    out_shape = [
        jax.ShapeDtypeStruct((lines, group, lanes), f32),
        jax.ShapeDtypeStruct((lines, group, lanes), f32),
        jax.ShapeDtypeStruct((lines, 3 * n * per), bf16),
        jax.ShapeDtypeStruct((2, 8, lanes), f32),
    ]
    out_specs = [vmem, vmem, vmem, any_spec]
    if G > 1:
        out_shape.insert(0, jax.ShapeDtypeStruct((G - 1, lines, group, lanes), f32))
        out_specs.insert(0, any_spec)
    *done, raw, part, late, pair_out = pl.pallas_call(
        functools.partial(kernel, n, L, R, C, G),
        out_shape=out_shape,
        in_specs=[pl.BlockSpec(memory_space=pltpu.SMEM)] + [hbm] * 8,
        out_specs=out_specs,
        scratch_shapes=[
            *(pltpu.SMEM(a.shape, a.dtype) for a in args[:3]),
            pltpu.VMEM((4, lines, lines), f32),
            pltpu.VMEM((lines, lines), bf16),
            pltpu.VMEM((G, lines, group, lanes), f32),
            pltpu.VMEM((G, lines, group, lanes), f32),
            pltpu.VMEM((L, n, R, lanes), f32),
            pltpu.VMEM((L, half, lanes), f32),
            pltpu.VMEM((L, half, 2 * lanes), f32),
            pltpu.VMEM((L, half, lanes), f32),
            pltpu.VMEM((L, 2 * half, lanes), f32),
            pltpu.VMEM((L, n, R, lanes), f32),
            pltpu.VMEM((max(1, G - 1), lines, group, lanes), f32),
            pltpu.VMEM((5, lines, lines), bf16),
            pltpu.VMEM((5, lines, lines), bf16),
            pltpu.VMEM((2, lines, lines), bf16),
            pltpu.VMEM((lines, 3 * (lines - n * per)), bf16),
            pltpu.VMEM((2, 8, lanes), f32),
            dma((2,)),
            dma((3,)),
            dma((2,)),
            dma((C,)),
            dma,
            dma,
            dma((C,)),
            dma,
            dma((max(1, C - 1),)),
            dma((G,)),
            dma,
            dma,
            dma,
            dma,
            dma,
            dma,
        ],
        compiler_params=pltpu.CompilerParams(
            collective_id=0, has_side_effects=True, vmem_limit_bytes=42 << 20
        ),
    )(species, *(pltpu.with_memory_space_constraint(a, pltpu.HBM) for a in (*args, concentration)))

    return pl.pallas_call(
        functools.partial(last_kernel, [(d * L + L - per, per) for d in range(n)]),
        out_shape=whole,
        in_specs=[vmem] * 4 + [any_spec] * len(done),
        out_specs=hbm,
        scratch_shapes=[pltpu.VMEM((lines, group, lanes), f32), dma((G,))],
        compiler_params=pltpu.CompilerParams(vmem_limit_bytes=8 << 20),
    )(late, pair_out, raw, part, *done)


def solution(mesh):
    in_specs = (P("groups", "row", "col"), P("groups"), P(), P(), P(), P(), P(), P(), P())
    out_specs = P("groups", "row", "col")
    return jax.shard_map(
        functools.partial(on_device, mesh.shape["row"]),
        mesh=mesh, in_specs=in_specs, out_specs=out_specs, check_vma=False,
    )
```
